512 devices in a mesh: dp: 64 (over z, y), section: 2 (over core), mp: 4 (over x).
Axes of the slice: x: 4, y: 4, z: 16, core: 2. Of those that a mesh axis runs over, the one named last changes fastest.
Arguments:
- frames: bfloat16 [64, 128, 512], P('dp'), may hold values from -6 to 6
- lengths: int32 [64], P('dp'), may hold values from 32 to 128
- feature_proj: bfloat16 [512, 1920], P(None, 'mp'), may hold values from -0.25 to 0.25
- norm_gain: float32 [2, 1920], P('section'), may hold values from 0.25 to 1.75
- qkv_weight: bfloat16 [2, 1920, 5760], P('section', 'dp', 'mp'), may hold values from -0.125 to 0.125
- out_weight: bfloat16 [2, 1920, 1920], P('section', 'mp', 'dp'), may hold values from -0.125 to 0.125
- center: float32 [1920], replicated, may hold values from -4 to 4
- whitening: float32 [1920, 1024], P(None, 'dp'), may hold values from -0.125 to 0.125
Outputs:
- embeddings: float32 [64, 1024], P(None, 'dp')
The draws below stay inside these ranges and needn't reach their ends.
All inputs are finite; a program needn't handle non-finite values.
Results may differ from the reference program's by a relative error of at most 0.0095.
Values may be sent and summed in bfloat16 or wider, within the bound.
No kernel may reach another device: no remote copies, remote signals or barrier semaphores. Data moves between devices by JAX's collectives and lax.ppermute only.
A program may use at most 64 MiB of HBM per device.

```python
import jax
import jax.numpy as jnp
from jax import lax

D = 1920
H = 16
HD = 120
CIN = 512
OUT = 1024
F = 128
UTTS = 64
N_MP = 4


def with_ends(array, rng, smallest, largest):
    longest = array.shape.index(max(array.shape))
    spots = []
    for shift in (0, 1):
        where = [jax.random.randint(jax.random.fold_in(rng, axis), (), 0, length) for axis, length in enumerate(array.shape)]
        where[longest] = (where[longest] + shift) % array.shape[longest]
        spots.append(tuple(where))
    return array.at[spots[0]].set(smallest).at[spots[1]].set(largest)


def levels(key, shape, cuts, smallest, top_value):
    level, own = 1.0, jax.random.fold_in(key, 6)
    for position, blocks in cuts:
        heights = jnp.exp(jax.random.uniform(jax.random.fold_in(own, position), (blocks,), jnp.float32, smallest / len(cuts), top_value / len(cuts)))
        level = level * jnp.repeat(heights, shape[position] // blocks).reshape([-1 if axis == position else 1 for axis in range(len(shape))])
    return level


def noise(rng, extent, deviation, reach, pieces=(), kind=jnp.bfloat16):
    level = levels(rng, extent, pieces, -0.22, 0.18) if pieces else 1.0
    drawn = jax.random.normal(rng, extent, jnp.float32) * deviation * level
    return jnp.minimum(jnp.maximum(drawn, -reach), reach).astype(kind)


def setup_inputs(seed: int = 0) -> dict:
    splits = jax.random.split(jax.random.key(seed), 9)
    return {
        "frames": noise(splits[0], (UTTS, F, CIN), 1.0, 6.0, ((0, 64),)),
        "lengths": with_ends(jax.random.randint(splits[1], (UTTS,), F // 4, F + 1), jax.random.fold_in(splits[1], 1), F // 4, F).astype(jnp.int32),
        "feature_proj": noise(splits[2], (CIN, D), CIN ** -0.5, 0.25, ((1, 4),)),
        "norm_gain": jnp.clip(1.0 + 0.15 * jax.random.normal(splits[3], (2, D), jnp.float32), 0.25, 1.75),
        "qkv_weight": noise(splits[4], (2, D, 3 * D), D ** -0.5, 0.125, ((0, 2), (1, 64), (2, 4))),
        "out_weight": noise(splits[5], (2, D, D), D ** -0.5, 0.125, ((0, 2), (1, 4), (2, 64))),
        "center": noise(splits[6], (D,), 1.0, 4.0, (), jnp.float32),
        "whitening": noise(splits[7], (D, OUT), D ** -0.5, 0.125, ((1, 64),), jnp.float32),
    }


def layer_norm(values, gain):
    mean = lax.optimization_barrier(jnp.mean(values, axis=-1, keepdims=True))
    centered = values - mean
    var = lax.optimization_barrier(jnp.mean(centered * centered, axis=-1, keepdims=True))
    return centered * lax.rsqrt(var + 1e-05) * gain

def attention_layer(x, length, gain, qkv_weight, out_weight):
    frames_count = x.shape[0]
    heads_local = H // N_MP
    normed = layer_norm(x.astype(jnp.float32), gain).astype(jnp.bfloat16)
    qkv = jnp.dot(normed, qkv_weight, preferred_element_type=jnp.float32).astype(jnp.bfloat16)
    qkv = qkv.reshape(frames_count, N_MP, 3, heads_local, HD).astype(jnp.float32)
    query = qkv[:, :, 0]
    keys = qkv[:, :, 1]
    values = qkv[:, :, 2]
    scores = jnp.einsum('qghd,kghd->ghqk', query, keys) / jnp.sqrt(jnp.float32(HD))
    valid = jnp.arange(frames_count, dtype=jnp.int32) < length
    scores = jnp.where(valid[None, None, None, :], scores, jnp.float32(-1e+30))
    probs = jax.nn.softmax(scores, axis=-1).astype(jnp.bfloat16).astype(jnp.float32)
    context = jnp.einsum('ghqk,kghd->qghd', probs, values).astype(jnp.bfloat16)
    context = context.reshape(frames_count, N_MP, heads_local * HD).astype(jnp.float32)
    grouped_out = out_weight.reshape(N_MP, heads_local * HD, D).astype(jnp.float32)
    partials = jnp.einsum('qgc,gcd->gqd', context, grouped_out).astype(jnp.bfloat16)
    attended = lax.optimization_barrier(jnp.sum(partials.astype(jnp.float32), axis=0))
    return (x.astype(jnp.float32) + attended).astype(jnp.bfloat16)

def reference(frames, lengths, feature_proj, norm_gain, qkv_weight, out_weight, center, whitening):

    def one_utterance(item):
        feats, length = item
        hidden = jnp.dot(feats, feature_proj, preferred_element_type=jnp.float32).astype(jnp.bfloat16)
        for layer_index in range(2):
            hidden = attention_layer(hidden, length, norm_gain[layer_index], qkv_weight[layer_index], out_weight[layer_index])
        valid = jnp.arange(hidden.shape[0], dtype=jnp.int32) < length
        summed = lax.optimization_barrier(jnp.sum(jnp.where(valid[:, None], hidden.astype(jnp.float32), jnp.float32(0.0)), axis=0))
        return summed / length.astype(jnp.float32)
    pooled = lax.map(one_utterance, (frames, lengths))
    return jnp.dot(pooled - center, whitening, precision=lax.Precision.HIGHEST, preferred_element_type=jnp.float32)
```

```python
import jax
import jax.numpy as jnp
from jax import lax
from jax.sharding import Mesh, PartitionSpec as P

HD = 120
NY = 4
BF = jnp.bfloat16
F32 = jnp.float32


def plane_gather(block):
    count = lax.axis_size("x") * lax.axis_size("y")
    spread = jnp.broadcast_to(block[None], (count,) + block.shape)
    return lax.all_to_all(spread, ("x", "y"), 0, 0)


def swap_cores(value):
    return lax.ppermute(value, "c", [(0, 1), (1, 0)])


def normalized(chunks, gain):
    values = chunks.astype(F32)
    width = values.shape[0] * values.shape[2]
    mean = jnp.sum(values, axis=(0, 2), keepdims=True) / width
    centered = values - mean
    var = jnp.sum(centered * centered, axis=(0, 2), keepdims=True) / width
    return (centered * lax.rsqrt(var + 1e-05) * gain[:, None, :]).astype(BF)


def head_probs(normed, q_weight, k_weight, v_weight, valid):
    def project(weight):
        return jnp.einsum(
            "btk,bkn->tn", normed, weight, preferred_element_type=F32
        ).astype(BF).reshape(2, 128, HD)

    query, keys, values = project(q_weight), project(k_weight), project(v_weight)
    scores = jnp.einsum("uqd,ukd->uqk", query, keys, preferred_element_type=F32)
    scores = scores / jnp.sqrt(F32(HD))
    scores = jnp.where(valid[:, None, :], scores, F32(-1e30))
    return jax.nn.softmax(scores, axis=-1).astype(BF), values


def body(frames, lengths, feature_proj, norm_gain, qkv_weight, out_weight, center, whitening):
    core = lax.axis_index("c")
    chunk = lax.axis_index("x") * NY + lax.axis_index("y")
    half = frames.shape[1] // 2

    qkv = qkv_weight[0].reshape(30, 3, NY, HD).transpose(2, 1, 0, 3)
    out = out_weight[0].T.reshape(30, NY, HD).transpose(1, 0, 2)[:, None]
    mats = jnp.concatenate([qkv, out], axis=1)
    tail = jnp.broadcast_to(lengths[0].astype(BF), (NY, 4, 2, HD))
    mats = jnp.concatenate([mats, tail], axis=2).reshape(2 * NY, 2, 32, HD)
    regrouped = lax.all_to_all(mats, ("y", "c"), 0, 0).reshape(NY, 2, 2, 32, HD)
    plane_lengths = regrouped[:, 0, 0, 30, 0].astype(jnp.int32)

    def layer_weights(layer):
        shard = regrouped[:, layer, :, :30].transpose(1, 0, 2, 3).reshape(2, HD, HD)
        shard = jnp.pad(shard, ((0, 0), (0, 8), (0, 8)))
        return lax.all_gather(shard, "z", axis=0)

    halves = [layer_weights(0), layer_weights(1)]

    def both_halves(own):
        own = own[:, :, :HD, :HD]
        other = swap_cores(own)
        first = jnp.where(core == 0, own, other)
        second = jnp.where(core == 0, other, own)
        return first[:, 0], first[:, 1], second[:, 0], second[:, 1]

    own_half = lax.dynamic_slice_in_dim(frames[0], core * half, half, 0)
    projected = jnp.dot(own_half, feature_proj, preferred_element_type=F32).astype(BF)
    projected = projected.reshape(half, NY, HD).transpose(1, 0, 2)
    plane = plane_gather(projected).reshape(4, NY, NY, half, HD)
    plane = plane.transpose(1, 0, 2, 3, 4).reshape(NY, 16, half, HD)
    mine = lax.dynamic_slice_in_dim(plane, 2 * core, 2, 0)
    theirs = lax.dynamic_slice_in_dim(plane, 2 * (1 - core), 2, 0)
    theirs = swap_cores(theirs)
    x0 = jnp.stack([mine, theirs], axis=1).transpose(2, 0, 1, 3, 4).reshape(16, 256, HD)

    gains = lax.all_gather(norm_gain[0], "c", axis=0).reshape(2, 16, HD)
    frame_ids = jnp.concatenate(
        [core * half + jnp.arange(half), (1 - core) * half + jnp.arange(half)]
    )
    my_lengths = lax.dynamic_slice_in_dim(plane_lengths, 2 * core, 2, 0)
    valid = frame_ids[None, :] < my_lengths[:, None]
    share = valid.astype(F32) / my_lengths.astype(F32)[:, None]

    white_cols = lax.all_gather(whitening.T, "y", axis=0, tiled=True).reshape(64, 16, HD)

    q_w, k_w, v_w, o_w = both_halves(halves[0])
    probs, values = head_probs(normalized(x0, gains[0]), q_w, k_w, v_w, valid)
    context = jnp.einsum("uqk,ukd->uqd", probs, values, preferred_element_type=F32)
    context = context.astype(BF).reshape(256, HD)
    partial = jnp.einsum("tr,bcr->btc", context, o_w, preferred_element_type=F32).astype(BF)
    partial = lax.all_to_all(partial, ("x", "y"), 0, 0)
    attended = jnp.sum(partial.astype(F32), axis=0)
    x0_own = lax.dynamic_index_in_dim(x0, chunk, 0, keepdims=False)
    x1_own = (x0_own.astype(F32) + attended).astype(BF)
    x1 = plane_gather(x1_own)

    q_w, k_w, v_w, o_w = both_halves(halves[1])
    probs, values = head_probs(normalized(x1, gains[1]), q_w, k_w, v_w, valid)
    context = jnp.einsum("uqk,ukd->uqd", probs, values, preferred_element_type=F32).astype(BF)
    pooled_context = jnp.sum(context.astype(F32) * share[:, :, None], axis=1)
    pooled_x1 = jnp.sum(x1_own.reshape(2, 128, HD).astype(F32) * share[:, :, None], axis=1)
    out_white = jnp.einsum(
        "nbc,bcr->nr", white_cols, o_w.astype(F32), precision=lax.Precision.HIGHEST
    )
    white_own = lax.dynamic_index_in_dim(white_cols, chunk, 1, keepdims=False)
    center_own = lax.dynamic_index_in_dim(center.reshape(16, HD), chunk, 0, keepdims=False)
    packed = jnp.concatenate([pooled_context, pooled_x1 - center_own], axis=1)
    packed = jnp.broadcast_to(packed[None], (16,) + packed.shape)
    packed = lax.all_to_all(packed, "z", 0, 0).reshape(32, 2 * HD)
    mixed = jnp.concatenate([out_white, white_own], axis=1)
    part = jnp.einsum("tk,nk->nt", packed, mixed, precision=lax.Precision.HIGHEST)
    part = jnp.broadcast_to(part.reshape(NY, 1, 16, 32), (NY, 8, 16, 32)).reshape(32, 16, 32)
    part = lax.all_to_all(part, ("y", "c", "x"), 0, 0).reshape(NY, 2, 4, 16, 32)
    total = jnp.sum(part, axis=(0, 2))
    return total.reshape(2, 16, 16, 2).transpose(2, 0, 3, 1).reshape(64, 16)


def solution(mesh):
    devices = mesh.devices.reshape(-1, NY, 2, 4)
    split = Mesh(devices, ("z", "y", "c", "x"))
    dp = ("z", "y")
    in_specs = (
        P(dp, None, None),
        P(dp),
        P(None, "x"),
        P("c", None),
        P("c", dp, "x"),
        P("c", "x", dp),
        P(),
        P(None, dp),
    )
    return jax.shard_map(
        body, mesh=split, in_specs=in_specs, out_specs=P(None, dp), check_vma=False
    )
```

```python
import jax
import jax.numpy as jnp
from jax import lax
from jax.sharding import Mesh, PartitionSpec as P

HD = 120
NY = 4
BF = jnp.bfloat16
F32 = jnp.float32


def plane_gather(block):
    count = lax.axis_size("x") * lax.axis_size("y")
    spread = jnp.broadcast_to(block[None], (count,) + block.shape)
    return lax.all_to_all(spread, ("x", "y"), 0, 0)


def swap_cores(value):
    return lax.ppermute(value, "c", [(0, 1), (1, 0)])


def normalized(chunks, gain):
    values = chunks.astype(F32)
    width = values.shape[0] * values.shape[2]
    mean = jnp.sum(values, axis=(0, 2), keepdims=True) / width
    centered = values - mean
    var = jnp.sum(centered * centered, axis=(0, 2), keepdims=True) / width
    return (centered * lax.rsqrt(var + 1e-05) * gain[:, None, :]).astype(BF)


def head_probs(normed, q_weight, k_weight, v_weight, valid):
    def project(weight):
        return jnp.einsum(
            "btk,bkn->tn", normed, weight, preferred_element_type=F32
        ).astype(BF).reshape(2, 128, HD)

    query, keys, values = project(q_weight), project(k_weight), project(v_weight)
    scores = jnp.einsum("uqd,ukd->uqk", query, keys, preferred_element_type=F32)
    scores = scores / jnp.sqrt(F32(HD))
    scores = jnp.where(valid[:, None, :], scores, F32(-1e30))
    return jax.nn.softmax(scores, axis=-1).astype(BF), values


def body(frames, lengths, feature_proj, norm_gain, qkv_weight, out_weight, center, whitening):
    core = lax.axis_index("c")
    chunk = lax.axis_index("x") * NY + lax.axis_index("y")
    half = frames.shape[1] // 2

    qkv = qkv_weight[0].reshape(30, 3, NY, HD).transpose(2, 1, 0, 3)
    out = out_weight[0].T.reshape(30, NY, HD).transpose(1, 0, 2)[:, None]
    mats = jnp.concatenate([qkv, out], axis=1)
    tail = jnp.broadcast_to(lengths[0].astype(BF), (NY, 4, 2, HD))
    mats = jnp.concatenate([mats, tail], axis=2)
    mats = jnp.broadcast_to(mats[:, None], (NY, 2, 4, 32, HD)).reshape(2 * NY, 4, 32, HD)
    regrouped = lax.all_to_all(mats, ("y", "c"), 0, 0).reshape(NY, 2, 4, 32, HD)
    plane_lengths = regrouped[:, 0, 0, 30, 0].astype(jnp.int32)

    def shard(layer):
        rows = regrouped[:, layer, :, :30].transpose(1, 0, 2, 3)
        return rows.reshape(4, HD, HD)

    first_shard = lax.dynamic_slice_in_dim(shard(0), 2 * core, 2, 0)
    first_shard, second_shard = lax.optimization_barrier((first_shard, shard(1)))
    second_weights = lax.all_gather(second_shard, "z", axis=0)
    own = lax.all_gather(first_shard, "z", axis=0)

    def both_halves(own):
        other = swap_cores(own)
        first = jnp.where(core == 0, own, other)
        second = jnp.where(core == 0, other, own)
        return first[:, 0], first[:, 1], second[:, 0], second[:, 1]

    own_half = lax.dynamic_slice_in_dim(frames[0], core * half, half, 0)
    projected = jnp.dot(own_half, feature_proj, preferred_element_type=F32).astype(BF)
    projected = projected.reshape(half, NY, HD).transpose(1, 0, 2)
    plane = plane_gather(projected).reshape(4, NY, NY, half, HD)
    plane = plane.transpose(1, 0, 2, 3, 4).reshape(NY, 16, half, HD)
    mine = lax.dynamic_slice_in_dim(plane, 2 * core, 2, 0)
    theirs = lax.dynamic_slice_in_dim(plane, 2 * (1 - core), 2, 0)
    theirs = swap_cores(theirs)
    x0 = jnp.stack([mine, theirs], axis=1).transpose(2, 0, 1, 3, 4).reshape(16, 256, HD)

    gains = lax.all_gather(norm_gain[0], "c", axis=0).reshape(2, 16, HD)
    frame_ids = jnp.concatenate(
        [core * half + jnp.arange(half), (1 - core) * half + jnp.arange(half)]
    )
    my_lengths = lax.dynamic_slice_in_dim(plane_lengths, 2 * core, 2, 0)
    valid = frame_ids[None, :] < my_lengths[:, None]
    share = valid.astype(F32) / my_lengths.astype(F32)[:, None]

    white_cols = whitening.T.reshape(16, 16, HD).transpose(1, 0, 2)
    white_cols = jnp.broadcast_to(white_cols[None], (NY, 16, 16, HD))
    white_cols = lax.all_to_all(white_cols, "y", 0, 0)

    x0, white_cols, gains = lax.optimization_barrier((x0, white_cols, gains))

    q_w, k_w, v_w, o_w = both_halves(own)
    probs, values = head_probs(normalized(x0, gains[0]), q_w, k_w, v_w, valid)
    context = jnp.einsum("uqk,ukd->uqd", probs, values, preferred_element_type=F32)
    context = context.astype(BF).reshape(256, HD)
    partial = jnp.einsum("tr,bcr->btc", context, o_w, preferred_element_type=F32).astype(BF)
    partial = lax.all_to_all(partial, ("x", "y"), 0, 0)
    attended = jnp.sum(partial.astype(F32), axis=0)
    x0_own = lax.dynamic_index_in_dim(x0, chunk, 0, keepdims=False)
    x1_own = (x0_own.astype(F32) + attended).astype(BF)
    x1 = plane_gather(x1_own)

    q_w, k_w, v_w, o_w = (second_weights[:, i] for i in range(4))
    probs, values = head_probs(normalized(x1, gains[1]), q_w, k_w, v_w, valid)
    context = jnp.einsum("uqk,ukd->uqd", probs, values, preferred_element_type=F32).astype(BF)
    pooled_context = jnp.sum(context.astype(F32) * share[:, :, None], axis=1)
    pooled_x1 = jnp.sum(x1_own.reshape(2, 128, HD).astype(F32) * share[:, :, None], axis=1)
    out_white = jnp.einsum(
        "ybnc,bcr->ynr", white_cols, o_w.astype(F32), precision=lax.Precision.HIGHEST
    )
    white_own = lax.dynamic_index_in_dim(white_cols, chunk, 1, keepdims=False)
    center_own = lax.dynamic_index_in_dim(center.reshape(16, HD), chunk, 0, keepdims=False)
    packed = jnp.concatenate([pooled_context, pooled_x1 - center_own], axis=1)
    packed = jnp.broadcast_to(packed[None], (16,) + packed.shape)
    packed = lax.all_to_all(packed, "z", 0, 0).reshape(32, 2 * HD)
    mixed = jnp.concatenate([out_white, white_own], axis=2).reshape(64, 2 * HD)
    part = jnp.einsum("tk,nk->nt", packed, mixed, precision=lax.Precision.HIGHEST)
    part = jnp.broadcast_to(part.reshape(NY, 1, 16, 32), (NY, 8, 16, 32)).reshape(32, 16, 32)
    part = lax.all_to_all(part, ("y", "c", "x"), 0, 0).reshape(NY, 2, 4, 16, 32)
    total = jnp.sum(part, axis=(0, 2))
    return total.reshape(2, 16, 16, 2).transpose(2, 0, 3, 1).reshape(64, 16)


def solution(mesh):
    devices = mesh.devices.reshape(-1, NY, 2, 4)
    split = Mesh(devices, ("z", "y", "c", "x"))
    dp = ("z", "y")
    in_specs = (
        P(dp, None, None),
        P(dp),
        P(None, "x"),
        P("c", None),
        P("c", dp, "x"),
        P("c", "x", dp),
        P(),
        P(None, dp),
    )
    return jax.shard_map(
        body, mesh=split, in_specs=in_specs, out_specs=P(None, dp), check_vma=False
    )
```

```python
import jax
import jax.numpy as jnp
from jax import lax
from jax.experimental import pallas as pl
from jax.experimental.pallas import tpu as pltpu
from jax.sharding import Mesh, PartitionSpec as P

HD = 120
NY = 4
CHUNKS = 16
BF = jnp.bfloat16
F32 = jnp.float32
VMEM = pl.BlockSpec(memory_space=pltpu.VMEM)
SMEM = pl.BlockSpec(memory_space=pltpu.SMEM)


def plane_gather(block):
    count = lax.axis_size("x") * lax.axis_size("y")
    spread = jnp.broadcast_to(block[None], (count,) + block.shape)
    return lax.all_to_all(spread, ("x", "y"), 0, 0)


def swap_cores(value):
    return lax.ppermute(value, "c", [(0, 1), (1, 0)])


def matmul(left, right, contract_right=0):
    return lax.dot_general(
        left, right, (((1,), (contract_right,)), ((), ())), preferred_element_type=F32
    )


def normalize(values, gain, along):
    values = values.astype(F32)
    width = CHUNKS * HD
    mean = jnp.sum(jnp.sum(values, axis=0, keepdims=True), axis=along, keepdims=True) / width
    centered = values - mean
    var = jnp.sum(jnp.sum(centered * centered, axis=0, keepdims=True), axis=along, keepdims=True)
    return (centered * lax.rsqrt(var / width + 1e-05) * gain).astype(BF)


def project(normed_ref, weight_ref, index, out_ref, slot, contract):
    total = jnp.zeros((HD, 256), F32)
    for b in range(CHUNKS):
        total += matmul(weight_ref[b, index], normed_ref[b], contract)
    out_ref[slot] = total.astype(BF)


def frame_of(place, core):
    return jnp.where(place < 64, place + core * 64, place - core * 64)


def attend(qkv_ref, u, core, length):
    columns = slice(u * 128, u * 128 + 128)
    keys = qkv_ref[1, :, columns].astype(F32).T.astype(BF)
    scores = matmul(keys, qkv_ref[0, :, columns]) / jnp.sqrt(F32(HD))
    place = lax.broadcasted_iota(jnp.int32, (128, 128), 0)
    scores = jnp.where(frame_of(place, core) < length, scores, F32(-1e30))
    top = jnp.max(scores, axis=0, keepdims=True)
    grown = jnp.exp(scores - top)
    probs = (grown / jnp.sum(grown, axis=0, keepdims=True)).astype(BF)
    return matmul(qkv_ref[2, :, columns], probs).astype(BF)


def first_kernel(scalars, raw, swapped, own, other, gain, partial, kept, normed, qkv, context):
    core = scalars[0]
    xi, yi = scalars[1], scalars[2]
    for u in range(2):
        for h in range(2):
            rows = slice(u * 128 + h * 64, u * 128 + h * 64 + 64)
            picks = [raw[x, 2 * core + u] if h == 0 else swapped[x, u] for x in range(4)]
            values = jnp.concatenate(picks, axis=0)
            normed[:, rows, :] = normalize(values, gain[...], 2)
        low = raw[xi, 2 * core + u, yi].astype(F32)
        high = swapped[xi, u, yi].astype(F32)
        both = jnp.concatenate([low, high], axis=0)
        kept[:, u * 128 : u * 128 + 128] = both.T.astype(BF)

    def qkv_from(low, high):
        project(normed, low, 0, qkv, 0, 1)
        project(normed, low, 1, qkv, 1, 1)
        project(normed, high, 0, qkv, 2, 1)

    def out_from(high):
        for b in range(CHUNKS):
            partial[b] = matmul(high[b, 1], context[...]).astype(BF)

    pl.when(core == 0)(lambda: qkv_from(own, other))
    pl.when(core == 1)(lambda: qkv_from(other, own))
    for u in range(2):
        context[:, u * 128 : u * 128 + 128] = attend(qkv, u, core, scalars[3 + u])
    pl.when(core == 0)(lambda: out_from(other))
    pl.when(core == 1)(lambda: out_from(own))


def second_kernel(scalars, x1, weights, gain, pooled, normed, qkv):
    core = scalars[0]
    for part in range(2):
        columns = slice(part * 128, part * 128 + 128)
        normed[:, :, columns] = normalize(x1[:, :, columns], gain[...], 1)
    for index in range(3):
        project(normed, weights, index, qkv, index, 0)
    for u in range(2):
        length = scalars[3 + u]
        context = attend(qkv, u, core, length).astype(F32)
        place = lax.broadcasted_iota(jnp.int32, (HD, 128), 1)
        valid = frame_of(place, core) < length
        total = jnp.sum(jnp.where(valid, context, F32(0.0)), axis=1, keepdims=True)
        pooled[:, u : u + 1] = total / length.astype(F32)


def run_first(scalars, raw, swapped, own, other, gain):
    return pl.pallas_call(
        first_kernel,
        out_shape=(
            jax.ShapeDtypeStruct((CHUNKS, HD, 256), BF),
            jax.ShapeDtypeStruct((HD, 256), BF),
        ),
        in_specs=[SMEM] + [VMEM] * 5,
        out_specs=(VMEM, VMEM),
        scratch_shapes=[
            pltpu.VMEM((CHUNKS, 256, HD), BF),
            pltpu.VMEM((3, HD, 256), BF),
            pltpu.VMEM((HD, 256), BF),
        ],
        compiler_params=pltpu.CompilerParams(vmem_limit_bytes=20 << 20),
        cost_estimate=pl.CostEstimate(
            flops=1_000_000_000, bytes_accessed=6_000_000, transcendentals=32768
        ),
        name="first_layer",
    )(scalars, raw, swapped, own, other, gain)


def run_second(scalars, x1, weights, gain):
    return pl.pallas_call(
        second_kernel,
        out_shape=jax.ShapeDtypeStruct((HD, 2), F32),
        in_specs=[SMEM] + [VMEM] * 3,
        out_specs=VMEM,
        scratch_shapes=[
            pltpu.VMEM((CHUNKS, HD, 256), BF),
            pltpu.VMEM((3, HD, 256), BF),
        ],
        compiler_params=pltpu.CompilerParams(vmem_limit_bytes=20 << 20),
        cost_estimate=pl.CostEstimate(
            flops=1_000_000_000, bytes_accessed=6_000_000, transcendentals=32768
        ),
        name="second_layer",
    )(scalars, x1, weights, gain)


def body(frames, lengths, feature_proj, norm_gain, qkv_weight, out_weight, center, whitening):
    core = lax.axis_index("c")
    xi, yi = lax.axis_index("x"), lax.axis_index("y")
    chunk = xi * NY + yi
    half = frames.shape[1] // 2

    qkv = qkv_weight[0].reshape(30, 3, NY, HD).transpose(2, 1, 0, 3)
    out = out_weight[0].T.reshape(30, NY, HD).transpose(1, 0, 2)[:, None]
    mats = jnp.concatenate([qkv, out], axis=1)
    tail = jnp.broadcast_to(lengths[0].astype(BF), (NY, 4, 2, HD))
    mats = jnp.concatenate([mats, tail], axis=2)
    mats = jnp.broadcast_to(mats[:, None], (NY, 2, 4, 32, HD)).reshape(2 * NY, 4, 32, HD)
    regrouped = lax.all_to_all(mats, ("y", "c"), 0, 0).reshape(NY, 2, 4, 32, HD)
    plane_lengths = regrouped[:, 0, 0, 30, 0].astype(jnp.int32)
    my_lengths = lax.dynamic_slice_in_dim(plane_lengths, 2 * core, 2, 0)
    gains = lax.all_gather(norm_gain[0], "c", axis=0)

    def shard(layer):
        rows = regrouped[:, layer, :, :30].transpose(1, 0, 2, 3).reshape(4, HD, HD)
        return jnp.concatenate([rows[:3].transpose(0, 2, 1), rows[3:]], axis=0)

    first_shard = lax.dynamic_slice_in_dim(shard(0), 2 * core, 2, 0)
    first_shard, second_shard, gains, my_lengths = lax.optimization_barrier(
        (first_shard, shard(1), gains, my_lengths)
    )
    second_weights = lax.all_gather(second_shard, "z", axis=0)
    own = lax.all_gather(first_shard, "z", axis=0)
    other = swap_cores(own)

    own_half = lax.dynamic_slice_in_dim(frames[0], core * half, half, 0)
    projected = jnp.dot(own_half, feature_proj, preferred_element_type=F32).astype(BF)
    projected = projected.reshape(half, NY, HD).transpose(1, 0, 2)
    raw = plane_gather(projected).reshape(4, NY, NY, half, HD)
    theirs = lax.dynamic_slice_in_dim(raw, 2 * (1 - core), 2, 1)
    swapped = swap_cores(theirs)

    scalars = jnp.concatenate([jnp.stack([core, xi, yi]).astype(jnp.int32), my_lengths])
    first_gain = gains[0].reshape(CHUNKS, 1, HD)
    second_gain = gains[1].reshape(CHUNKS, HD, 1)
    partial, x0_own = run_first(scalars, raw, swapped, own, other, first_gain)

    white = whitening.T.reshape(16, CHUNKS, HD).transpose(1, 0, 2)
    partial, white = lax.optimization_barrier((partial, white))
    whites = [white]
    for step in range(1, NY):
        pairs = [((i + step) % NY, i) for i in range(NY)]
        whites.append(lax.ppermute(white, "y", pairs))

    partial = lax.all_to_all(partial, ("x", "y"), 0, 0)
    attended = jnp.sum(partial.astype(F32), axis=0)
    x1_own = (x0_own.astype(F32) + attended).astype(BF)
    x1 = plane_gather(x1_own)

    frame_ids = jnp.concatenate(
        [core * half + jnp.arange(half), (1 - core) * half + jnp.arange(half)]
    )
    valid = frame_ids[None, :] < my_lengths[:, None]
    share = valid.astype(F32) / my_lengths.astype(F32)[:, None]
    pooled_x1 = jnp.sum(x1_own.reshape(HD, 2, 128).astype(F32) * share, axis=2).T
    white_cols = jnp.concatenate([w[None] for w in whites], axis=0)
    out_white = jnp.einsum(
        "ybnc,bcr->ynr",
        white_cols,
        second_weights[:, 3].astype(F32),
        precision=lax.Precision.HIGHEST,
    )
    white_own = lax.dynamic_index_in_dim(white_cols, chunk, 1, keepdims=False)
    mixed = jnp.concatenate([out_white, white_own], axis=2)
    mixed = jnp.concatenate([mixed, mixed], axis=0)
    mixed = lax.dynamic_slice_in_dim(mixed, (NY - yi) % NY, NY, 0).reshape(64, 2 * HD)

    pooled_context = run_second(scalars, x1, second_weights, second_gain).T
    center_own = lax.dynamic_index_in_dim(center.reshape(CHUNKS, HD), chunk, 0, keepdims=False)
    packed = jnp.concatenate([pooled_context, pooled_x1 - center_own], axis=1)
    packed = jnp.broadcast_to(packed[None], (16,) + packed.shape)
    packed = lax.all_to_all(packed, "z", 0, 0).reshape(32, 2 * HD)
    part = jnp.einsum("tk,nk->nt", packed, mixed, precision=lax.Precision.HIGHEST)
    part = jnp.broadcast_to(part.reshape(NY, 1, 16, 32), (NY, 8, 16, 32)).reshape(32, 16, 32)
    part = lax.all_to_all(part, ("y", "c", "x"), 0, 0).reshape(NY, 2, 4, 16, 32)
    total = jnp.sum(part, axis=(0, 2))
    return total.reshape(2, 16, 16, 2).transpose(2, 0, 3, 1).reshape(64, 16)


def solution(mesh):
    devices = mesh.devices.reshape(-1, NY, 2, 4)
    split = Mesh(devices, ("z", "y", "c", "x"))
    dp = ("z", "y")
    in_specs = (
        P(dp, None, None),
        P(dp),
        P(None, "x"),
        P("c", None),
        P("c", dp, "x"),
        P("c", "x", dp),
        P(),
        P(None, dp),
    )
    return jax.shard_map(
        body, mesh=split, in_specs=in_specs, out_specs=P(None, dp), check_vma=False
    )
```

```python
import jax
import jax.numpy as jnp
from jax import lax
from jax.experimental import pallas as pl
from jax.experimental.pallas import tpu as pltpu
from jax.sharding import Mesh, PartitionSpec as P

HD = 120
NY = 4
CHUNKS = 16
BF = jnp.bfloat16
F32 = jnp.float32
VMEM = pl.BlockSpec(memory_space=pltpu.VMEM)
SMEM = pl.BlockSpec(memory_space=pltpu.SMEM)


def plane_gather(block):
    count = lax.axis_size("x") * lax.axis_size("y")
    spread = jnp.broadcast_to(block[None], (count,) + block.shape)
    return lax.all_to_all(spread, ("x", "y"), 0, 0)


def swap_cores(value):
    return lax.ppermute(value, "c", [(0, 1), (1, 0)])


def matmul(left, right):
    return jnp.dot(left, right, preferred_element_type=F32)


def normalize(values, gain_rows, out_ref, columns):
    values = values.astype(F32)
    width = CHUNKS * HD
    mean = jnp.sum(jnp.sum(values, axis=0), axis=0, keepdims=True) / width
    centered = values - mean[None]
    var = jnp.sum(jnp.sum(centered * centered, axis=0), axis=0, keepdims=True) / width
    scale = lax.rsqrt(var + 1e-05)
    for b in range(CHUNKS):
        out_ref[b, :, columns] = (centered[b] * scale * gain_rows[:, b : b + 1]).astype(BF)


def project(normed_ref, weight_ref, index, out_ref, slot):
    total = jnp.zeros((HD, 256), F32)
    for b in range(CHUNKS):
        total += matmul(weight_ref[b, index], normed_ref[b])
    out_ref[slot] = total.astype(BF)


def attend(query, keys, values, length):
    keys = keys.astype(F32).T.astype(BF)
    scores = matmul(keys, query) / jnp.sqrt(F32(HD))
    place = lax.broadcasted_iota(jnp.int32, (128, 128), 0)
    scores = jnp.where(place < length, scores, F32(-1e30))
    top = jnp.max(scores, axis=0, keepdims=True)
    grown = jnp.exp(scores - top)
    probs = (grown / jnp.sum(grown, axis=0, keepdims=True)).astype(BF)
    return matmul(values, probs).astype(BF)


def utterance(u):
    return slice(u * 128, u * 128 + 128)


def norm_kernel(scalars, raw, own, gain, normed, mine):
    core = scalars[0]
    gain_rows = gain[...].T
    for u in range(2):
        picks = [raw[x, 2 * core + u] for x in range(4)]
        values = jnp.concatenate(picks, axis=0)
        normalize(values, gain_rows, normed, utterance(u))
    project(normed, own, 0, mine, 0)
    pl.when(core == 0)(lambda: project(normed, own, 1, mine, 1))


def attend_kernel(scalars, raw, normed, mine, own, other, partial, kept, rest, context):
    core = scalars[0]
    xi, yi = scalars[1], scalars[2]
    for u in range(2):
        kept[:, utterance(u)] = raw[xi, 2 * core + u, yi]

    def attend_all(query, keys, values):
        for u in range(2):
            columns = utterance(u)
            context[:, columns] = attend(
                query[:, columns], keys[:, columns], values[:, columns], scalars[3 + u]
            )

    def out_from(high):
        for b in range(CHUNKS):
            partial[b] = matmul(high[b, 1], context[...]).astype(BF)

    def on_first():
        project(normed, other, 0, rest, 0)
        attend_all(mine.at[0], mine.at[1], rest.at[0])
        out_from(other)

    def on_second():
        project(normed, other, 0, rest, 0)
        project(normed, other, 1, rest, 1)
        attend_all(rest.at[0], rest.at[1], mine.at[0])
        out_from(own)

    pl.when(core == 0)(on_first)
    pl.when(core == 1)(on_second)


def second_kernel(scalars, x1, weights_hbm, gain, pooled, weights, normed, qkv, arrived):
    copy = pltpu.make_async_copy(weights_hbm.at[:, pl.ds(0, 3)], weights, arrived)
    copy.start()
    gain_rows = gain[...].T
    for u in range(2):
        normalize(x1[:, :, utterance(u)], gain_rows, normed, utterance(u))
    copy.wait()
    for index in range(3):
        project(normed, weights, index, qkv, index)
    for u in range(2):
        length = scalars[3 + u]
        columns = utterance(u)
        context = attend(qkv[0, :, columns], qkv[1, :, columns], qkv[2, :, columns], length)
        valid = lax.broadcasted_iota(jnp.int32, (HD, 128), 1) < length
        total = jnp.where(valid, context.astype(F32), F32(0.0))
        pooled[:, u : u + 1] = jnp.sum(total, axis=1, keepdims=True) / length.astype(F32)


def cost(flops, moved):
    return pl.CostEstimate(flops=flops, bytes_accessed=moved, transcendentals=32768)


def run_norm(scalars, raw, own, gain):
    return pl.pallas_call(
        norm_kernel,
        out_shape=(
            jax.ShapeDtypeStruct((CHUNKS, HD, 256), BF),
            jax.ShapeDtypeStruct((2, HD, 256), BF),
        ),
        in_specs=[SMEM] + [VMEM] * 3,
        out_specs=(VMEM, VMEM),
        compiler_params=pltpu.CompilerParams(vmem_limit_bytes=20 << 20),
        cost_estimate=cost(400_000_000, 4_000_000),
        name="first_norm",
    )(scalars, raw, own, gain)


def run_attend(scalars, raw, normed, mine, own, other):
    return pl.pallas_call(
        attend_kernel,
        out_shape=(
            jax.ShapeDtypeStruct((CHUNKS, HD, 256), BF),
            jax.ShapeDtypeStruct((HD, 256), BF),
        ),
        in_specs=[SMEM] + [VMEM] * 5,
        out_specs=(VMEM, VMEM),
        scratch_shapes=[
            pltpu.VMEM((2, HD, 256), BF),
            pltpu.VMEM((HD, 256), BF),
        ],
        compiler_params=pltpu.CompilerParams(vmem_limit_bytes=20 << 20),
        cost_estimate=cost(600_000_000, 5_000_000),
        name="first_attend",
    )(scalars, raw, normed, mine, own, other)


def run_second(scalars, x1, weights, gain):
    return pl.pallas_call(
        second_kernel,
        out_shape=jax.ShapeDtypeStruct((HD, 2), F32),
        in_specs=[SMEM, VMEM, pl.BlockSpec(memory_space=pltpu.HBM), VMEM],
        out_specs=VMEM,
        scratch_shapes=[
            pltpu.VMEM((CHUNKS, 3, HD, HD), BF),
            pltpu.VMEM((CHUNKS, HD, 256), BF),
            pltpu.VMEM((3, HD, 256), BF),
            pltpu.SemaphoreType.DMA,
        ],
        compiler_params=pltpu.CompilerParams(vmem_limit_bytes=58 << 20),
        cost_estimate=cost(1_000_000_000, 6_000_000),
        name="second_layer",
    )(scalars, x1, weights, gain)


def body(frames, lengths, feature_proj, norm_gain, qkv_weight, out_weight, center, whitening):
    core = lax.axis_index("c")
    xi, yi = lax.axis_index("x"), lax.axis_index("y")
    chunk = xi * NY + yi

    white_cols = jnp.pad(whitening.T, ((0, 24), (0, 0)))
    white_cols = lax.all_gather(white_cols, "y", axis=0)[:, :16].reshape(NY, 16, CHUNKS, HD)

    projected = lax.dot_general(
        feature_proj, frames[0], (((0,), (1,)), ((), ())), preferred_element_type=F32
    )
    projected = projected.astype(BF).reshape(1, NY, HD, 128)
    projected = jnp.broadcast_to(projected, (16, NY, HD, 128))

    qkv = qkv_weight[0].reshape(30, 3, NY, HD).transpose(2, 1, 0, 3)
    out = out_weight[0].T.reshape(30, NY, HD).transpose(1, 0, 2)[:, None]
    mats = jnp.concatenate([qkv, out], axis=1)
    tail = jnp.broadcast_to(lengths[0].astype(BF), (NY, 4, 2, HD))
    mats = jnp.concatenate([mats, tail], axis=2)
    mats = jnp.broadcast_to(mats[:, None], (NY, 2, 4, 32, HD)).reshape(2 * NY, 4, 32, HD)
    regrouped = lax.all_to_all(mats, ("y", "c"), 0, 0).reshape(NY, 2, 4, 32, HD)
    gains = lax.all_gather(norm_gain[0], "c", axis=0)
    regrouped, gains, projected = lax.optimization_barrier((regrouped, gains, projected))
    plane_lengths = regrouped[:, 0, 0, 30, 0].astype(jnp.int32)
    my_lengths = lax.dynamic_slice_in_dim(plane_lengths, 2 * core, 2, 0)

    def shard(layer):
        rows = regrouped[:, layer, :, :30].transpose(1, 0, 2, 3).reshape(4, HD, HD)
        return jnp.concatenate([rows[:3].transpose(0, 2, 1), rows[3:]], axis=0)

    first_shard = lax.dynamic_slice_in_dim(shard(0), 2 * core, 2, 0)
    first_shard, second_shard, my_lengths = lax.optimization_barrier(
        (first_shard, shard(1), my_lengths)
    )
    second_weights = lax.all_gather(second_shard, "z", axis=0)
    own = lax.all_gather(first_shard, "z", axis=0)
    other = swap_cores(own)

    raw = lax.all_to_all(projected, ("x", "y"), 0, 0).reshape(4, NY, NY, HD, 128)

    scalars = jnp.concatenate([jnp.stack([core, xi, yi]).astype(jnp.int32), my_lengths])
    gains = gains.reshape(2, CHUNKS, HD)
    normed, mine = run_norm(scalars, raw, own, gains[0])
    partial, x0_own = run_attend(scalars, raw, normed, mine, own, other)
    partial = lax.all_to_all(partial, ("x", "y"), 0, 0)
    attended = jnp.sum(partial.astype(F32), axis=0)
    x1_own = (x0_own.astype(F32) + attended).astype(BF)
    x1 = plane_gather(x1_own)

    valid = jnp.arange(128)[None, :] < my_lengths[:, None]
    share = valid.astype(F32) / my_lengths.astype(F32)[:, None]
    pooled_x1 = jnp.sum(x1_own.reshape(HD, 2, 128).astype(F32) * share, axis=2).T
    out_white = jnp.einsum(
        "ynbc,bcr->ynr",
        white_cols,
        second_weights[:, 3].astype(F32),
        precision=lax.Precision.HIGHEST,
    )
    white_own = lax.dynamic_index_in_dim(white_cols, chunk, 2, keepdims=False)
    mixed = jnp.concatenate([out_white, white_own], axis=2).reshape(64, 2 * HD)

    pooled_context = run_second(scalars, x1, second_weights, gains[1]).T
    center_own = lax.dynamic_index_in_dim(center.reshape(CHUNKS, HD), chunk, 0, keepdims=False)
    packed = jnp.concatenate([pooled_context, pooled_x1 - center_own], axis=1)
    packed = jnp.broadcast_to(packed[None], (16,) + packed.shape)
    packed = lax.all_to_all(packed, "z", 0, 0).reshape(32, 2 * HD)
    part = jnp.einsum("tk,nk->nt", packed, mixed, precision=lax.Precision.HIGHEST)
    part = jnp.broadcast_to(part.reshape(NY, 1, 16, 32), (NY, 8, 16, 32)).reshape(32, 16, 32)
    part = lax.all_to_all(part, ("y", "c", "x"), 0, 0).reshape(NY, 2, 4, 16, 32)
    total = jnp.sum(part, axis=(0, 2))
    return total.reshape(2, 16, 16, 2).transpose(2, 0, 3, 1).reshape(64, 16)


def solution(mesh):
    devices = mesh.devices.reshape(-1, NY, 2, 4)
    split = Mesh(devices, ("z", "y", "c", "x"))
    dp = ("z", "y")
    in_specs = (
        P(dp, None, None),
        P(dp),
        P(None, "x"),
        P("c", None),
        P("c", dp, "x"),
        P("c", "x", dp),
        P(),
        P(None, dp),
    )
    return jax.shard_map(
        body, mesh=split, in_specs=in_specs, out_specs=P(None, dp), check_vma=False
    )
```

```python
import jax
import jax.numpy as jnp
from jax import lax
from jax.experimental import pallas as pl
from jax.experimental.pallas import tpu as pltpu
from jax.sharding import Mesh, PartitionSpec as P

HD = 120
NY = 4
CHUNKS = 16
BF = jnp.bfloat16
F32 = jnp.float32
VMEM = pl.BlockSpec(memory_space=pltpu.VMEM)
SMEM = pl.BlockSpec(memory_space=pltpu.SMEM)


def plane_gather(block):
    count = lax.axis_size("x") * lax.axis_size("y")
    spread = jnp.broadcast_to(block[None], (count,) + block.shape)
    return lax.all_to_all(spread, ("x", "y"), 0, 0)


def swap_cores(value):
    return lax.ppermute(value, "c", [(0, 1), (1, 0)])


def matmul(left, right):
    return jnp.dot(left, right, preferred_element_type=F32)


def normalize(values, gain_rows, out_ref, columns):
    values = values.astype(F32)
    width = CHUNKS * HD
    mean = jnp.sum(jnp.sum(values, axis=0), axis=0, keepdims=True) / width
    centered = values - mean[None]
    var = jnp.sum(jnp.sum(centered * centered, axis=0), axis=0, keepdims=True) / width
    scale = lax.rsqrt(var + 1e-05)
    for b in range(CHUNKS):
        out_ref[b, :, columns] = (centered[b] * scale * gain_rows[:, b : b + 1]).astype(BF)


def project(normed_ref, weight_ref, index, out_ref, slot):
    total = jnp.zeros((HD, 256), F32)
    for b in range(CHUNKS):
        total += matmul(weight_ref[b, index], normed_ref[b])
    out_ref[slot] = total.astype(BF)


def attend(query, keys, values, length):
    keys = keys.astype(F32).T.astype(BF)
    scores = matmul(keys, query) / jnp.sqrt(F32(HD))
    place = lax.broadcasted_iota(jnp.int32, (128, 128), 0)
    scores = jnp.where(place < length, scores, F32(-1e30))
    top = jnp.max(scores, axis=0, keepdims=True)
    grown = jnp.exp(scores - top)
    probs = (grown / jnp.sum(grown, axis=0, keepdims=True)).astype(BF)
    return matmul(values, probs).astype(BF)


def utterance(u):
    return slice(u * 128, u * 128 + 128)


def norm_kernel(scalars, raw, own, gain, normed, mine):
    core = scalars[0]
    gain_rows = gain[...].T
    for u in range(2):
        picks = [raw[x, 2 * core + u] for x in range(4)]
        values = jnp.concatenate(picks, axis=0)
        normalize(values, gain_rows, normed, utterance(u))
    project(normed, own, 0, mine, 0)
    pl.when(core == 0)(lambda: project(normed, own, 1, mine, 1))


def attend_kernel(
    scalars, raw, normed, mine, own, other, partial, kept, rest, context
):
    core = scalars[0]
    xi, yi = scalars[1], scalars[2]
    for u in range(2):
        kept[:, utterance(u)] = raw[xi, 2 * core + u, yi]

    def attend_all(query, keys, values):
        for u in range(2):
            columns = utterance(u)
            context[:, columns] = attend(
                query[:, columns], keys[:, columns], values[:, columns], scalars[3 + u]
            )

    def out_from(high):
        for group in range(4):
            for b in range(4 * group, 4 * group + 4):
                partial[b] = matmul(high[b, 1], context[...]).astype(BF)

    def on_first():
        project(normed, other, 0, rest, 0)
        attend_all(mine.at[0], mine.at[1], rest.at[0])
        out_from(other)

    def on_second():
        project(normed, other, 0, rest, 0)
        project(normed, other, 1, rest, 1)
        attend_all(rest.at[0], rest.at[1], mine.at[0])
        out_from(own)

    pl.when(core == 0)(on_first)
    pl.when(core == 1)(on_second)


def stage_kernel(weights_hbm, staged, arrived):
    copy = pltpu.make_async_copy(weights_hbm.at[:, pl.ds(0, 3)], staged, arrived)
    copy.start()
    copy.wait()


def second_kernel(scalars, x1, weights, gain, rest, packed, normed, qkv):
    gain_rows = gain[...].T
    for u in range(2):
        normalize(x1[:, :, utterance(u)], gain_rows, normed, utterance(u))
    for index in range(3):
        project(normed, weights, index, qkv, index)
    for u in range(2):
        length = scalars[3 + u]
        columns = utterance(u)
        context = attend(qkv[0, :, columns], qkv[1, :, columns], qkv[2, :, columns], length)
        valid = lax.broadcasted_iota(jnp.int32, (128, HD), 0) < length
        total = jnp.where(valid, context.astype(F32).T, F32(0.0))
        pooled = jnp.sum(total, axis=0, keepdims=True) / length.astype(F32)
        row = jnp.concatenate([pooled, rest[u : u + 1, :]], axis=1)
        for z in range(16):
            packed[z, u : u + 1, :] = row


def cost(flops, moved):
    return pl.CostEstimate(flops=flops, bytes_accessed=moved, transcendentals=32768)


def run_norm(scalars, raw, own, gain):
    return pl.pallas_call(
        norm_kernel,
        out_shape=(
            jax.ShapeDtypeStruct((CHUNKS, HD, 256), BF),
            jax.ShapeDtypeStruct((2, HD, 256), BF),
        ),
        in_specs=[SMEM] + [VMEM] * 3,
        out_specs=(VMEM, VMEM),
        compiler_params=pltpu.CompilerParams(vmem_limit_bytes=20 << 20),
        cost_estimate=cost(400_000_000, 4_000_000),
        name="first_norm",
    )(scalars, raw, own, gain)


def run_attend(scalars, raw, normed, mine, own, other):
    return pl.pallas_call(
        attend_kernel,
        out_shape=(
            jax.ShapeDtypeStruct((CHUNKS, HD, 256), BF),
            jax.ShapeDtypeStruct((HD, 256), BF),
        ),
        in_specs=[SMEM] + [VMEM] * 5,
        out_specs=(VMEM, VMEM),
        scratch_shapes=[
            pltpu.VMEM((2, HD, 256), BF),
            pltpu.VMEM((HD, 256), BF),
        ],
        compiler_params=pltpu.CompilerParams(vmem_limit_bytes=20 << 20),
        cost_estimate=cost(600_000_000, 5_000_000),
        name="first_attend",
    )(scalars, raw, normed, mine, own, other)


def run_stage(weights):
    return pl.pallas_call(
        stage_kernel,
        out_shape=jax.ShapeDtypeStruct((CHUNKS, 3, HD, HD), BF),
        in_specs=[pl.BlockSpec(memory_space=pltpu.HBM)],
        out_specs=VMEM,
        scratch_shapes=[pltpu.SemaphoreType.DMA],
        compiler_params=pltpu.CompilerParams(vmem_limit_bytes=20 << 20),
        cost_estimate=cost(0, 3_000_000),
        name="stage",
    )(weights)


def run_second(scalars, x1, weights, gain, rest):
    return pl.pallas_call(
        second_kernel,
        out_shape=jax.ShapeDtypeStruct((16, 2, 2 * HD), F32),
        in_specs=[SMEM] + [VMEM] * 4,
        out_specs=VMEM,
        scratch_shapes=[
            pltpu.VMEM((CHUNKS, HD, 256), BF),
            pltpu.VMEM((3, HD, 256), BF),
        ],
        compiler_params=pltpu.CompilerParams(vmem_limit_bytes=20 << 20),
        cost_estimate=cost(1_000_000_000, 6_000_000),
        name="second_layer",
    )(scalars, x1, weights, gain, rest)


def body(frames, lengths, feature_proj, norm_gain, qkv_weight, out_weight, center, whitening):
    core = lax.axis_index("c")
    xi, yi = lax.axis_index("x"), lax.axis_index("y")
    chunk = xi * NY + yi

    projected = lax.dot_general(
        feature_proj, frames[0], (((0,), (1,)), ((), ())), preferred_element_type=F32
    )
    projected = projected.astype(BF).reshape(1, NY, HD, 128)
    projected = jnp.broadcast_to(projected, (16, NY, HD, 128))

    qkv = qkv_weight[0].reshape(30, 3, NY, HD).transpose(2, 1, 0, 3)
    out = out_weight[0].T.reshape(30, NY, HD).transpose(1, 0, 2)[:, None]
    mats = jnp.concatenate([qkv, out], axis=1)
    tail = jnp.broadcast_to(lengths[0].astype(BF), (NY, 4, 2, HD))
    mats = jnp.concatenate([mats, tail], axis=2)
    mats = jnp.broadcast_to(mats[:, None], (NY, 2, 4, 32, HD)).reshape(2 * NY, 4, 32, HD)
    regrouped = lax.all_to_all(mats, ("y", "c"), 0, 0).reshape(NY, 2, 4, 32, HD)
    gains = lax.all_gather(norm_gain[0], "c", axis=0)
    regrouped, gains, projected = lax.optimization_barrier((regrouped, gains, projected))
    plane_lengths = regrouped[:, 0, 0, 30, 0].astype(jnp.int32)
    my_lengths = lax.dynamic_slice_in_dim(plane_lengths, 2 * core, 2, 0)

    def shard(layer):
        rows = regrouped[:, layer, :, :30].transpose(1, 0, 2, 3).reshape(4, HD, HD)
        return jnp.concatenate([rows[:3].transpose(0, 2, 1), rows[3:]], axis=0)

    first_shard = lax.dynamic_slice_in_dim(shard(0), 2 * core, 2, 0)
    first_shard, second_shard, my_lengths = lax.optimization_barrier(
        (first_shard, shard(1), my_lengths)
    )
    second_weights = lax.all_gather(second_shard, "z", axis=0)
    own = lax.all_gather(first_shard, "z", axis=0)
    other = swap_cores(own)

    raw = lax.all_to_all(projected, ("x", "y"), 0, 0).reshape(4, NY, NY, HD, 128)

    scalars = jnp.concatenate([jnp.stack([core, xi, yi]).astype(jnp.int32), my_lengths])
    gains = gains.reshape(2, CHUNKS, HD)
    normed, mine = run_norm(scalars, raw, own, gains[0])
    partial, x0_own = run_attend(scalars, raw, normed, mine, own, other)
    white = whitening.T.reshape(16, CHUNKS, HD).transpose(1, 0, 2)
    x0_own, white = lax.optimization_barrier((x0_own, white))
    near = [(((y + 1 + c) % NY) * 2 + c, y * 2 + c) for y in range(NY) for c in range(2)]
    far = [(((y + 3) % NY) * 2 + 1, y * 2 + 1) for y in range(NY)]
    white_near = lax.ppermute(white, ("y", "c"), near)
    white_far = lax.ppermute(white, ("y", "c"), far)

    partial = lax.all_to_all(partial, ("x", "y"), 0, 0)
    attended = jnp.sum(partial.astype(F32), axis=0)
    x1_own = (x0_own.astype(F32) + attended).astype(BF)
    x1 = plane_gather(x1_own)

    valid = jnp.arange(128)[None, :] < my_lengths[:, None]
    share = valid.astype(F32) / my_lengths.astype(F32)[:, None]
    pooled_x1 = jnp.sum(x1_own.reshape(HD, 2, 128).astype(F32) * share, axis=2).T
    center_own = lax.dynamic_index_in_dim(center.reshape(CHUNKS, HD), chunk, 0, keepdims=False)
    staged = run_stage(second_weights)
    packed = run_second(scalars, x1, staged, gains[1], pooled_x1 - center_own)

    white_cols = jnp.stack(
        [jnp.where(core == 0, white, white_near), jnp.where(core == 0, white_near, white_far)]
    )
    out_white = jnp.einsum(
        "ybnc,bcr->ynr",
        white_cols,
        second_weights[:, 3].astype(F32),
        precision=lax.Precision.HIGHEST,
    )
    white_own = lax.dynamic_index_in_dim(white_cols, chunk, 1, keepdims=False)
    mixed = jnp.concatenate([out_white, white_own], axis=2)
    swapped = swap_cores(mixed)
    low = jnp.where(core == 0, mixed, swapped)
    high = jnp.where(core == 0, swapped, mixed)
    mixed = jnp.concatenate([low, high, low, high], axis=0)
    mixed = lax.dynamic_slice_in_dim(mixed, (NY - yi) % NY, NY, 0).reshape(64, 2 * HD)

    packed = lax.all_to_all(packed, "z", 0, 0).reshape(32, 2 * HD)
    part = jnp.einsum("tk,nk->nt", packed, mixed, precision=lax.Precision.HIGHEST)
    part = jnp.broadcast_to(part.reshape(NY, 1, 16, 32), (NY, 8, 16, 32)).reshape(32, 16, 32)
    part = lax.all_to_all(part, ("y", "c", "x"), 0, 0).reshape(NY, 2, 4, 16, 32)
    total = jnp.sum(part, axis=(0, 2))
    return total.reshape(2, 16, 16, 2).transpose(2, 0, 3, 1).reshape(64, 16)


def solution(mesh):
    devices = mesh.devices.reshape(-1, NY, 2, 4)
    split = Mesh(devices, ("z", "y", "c", "x"))
    dp = ("z", "y")
    in_specs = (
        P(dp, None, None),
        P(dp),
        P(None, "x"),
        P("c", None),
        P("c", dp, "x"),
        P("c", "x", dp),
        P(),
        P(None, dp),
    )
    return jax.shard_map(
        body, mesh=split, in_specs=in_specs, out_specs=P(None, dp), check_vma=False
    )
```

```python
import jax
import jax.numpy as jnp
from jax import lax
from jax.experimental import pallas as pl
from jax.experimental.pallas import tpu as pltpu
from jax.sharding import Mesh, PartitionSpec as P

HD = 120
NY = 4
CHUNKS = 16
BF = jnp.bfloat16
F32 = jnp.float32
VMEM = pl.BlockSpec(memory_space=pltpu.VMEM)
SMEM = pl.BlockSpec(memory_space=pltpu.SMEM)


def plane_gather(block):
    count = lax.axis_size("x") * lax.axis_size("y")
    spread = jnp.broadcast_to(block[None], (count,) + block.shape)
    return lax.all_to_all(spread, ("x", "y"), 0, 0)


def swap_cores(value):
    return lax.ppermute(value, "c", [(0, 1), (1, 0)])


def matmul(left, right):
    return jnp.dot(left, right, preferred_element_type=F32)


def normalize(values, gain_rows, out_ref, columns):
    values = values.astype(F32)
    width = CHUNKS * HD
    mean = jnp.sum(jnp.sum(values, axis=0), axis=0, keepdims=True) / width
    centered = values - mean[None]
    var = jnp.sum(jnp.sum(centered * centered, axis=0), axis=0, keepdims=True) / width
    scale = lax.rsqrt(var + 1e-05)
    for b in range(CHUNKS):
        out_ref[b, :, columns] = (centered[b] * scale * gain_rows[:, b : b + 1]).astype(BF)


def project(normed_ref, weight_ref, index, out_ref, slot):
    total = jnp.zeros((HD, 256), F32)
    for b in range(CHUNKS):
        total += matmul(weight_ref[b, index], normed_ref[b])
    out_ref[slot] = total.astype(BF)


def attend(query, keys, values, length):
    keys = keys.astype(F32).T.astype(BF)
    scores = matmul(keys, query) / jnp.sqrt(F32(HD))
    place = lax.broadcasted_iota(jnp.int32, (128, 128), 0)
    scores = jnp.where(place < length, scores, F32(-1e30))
    top = jnp.max(scores, axis=0, keepdims=True)
    grown = jnp.exp(scores - top)
    probs = (grown / jnp.sum(grown, axis=0, keepdims=True)).astype(BF)
    return matmul(values, probs).astype(BF)


def utterance(u):
    return slice(u * 128, u * 128 + 128)


def regroup_kernel(lengths, qkv, out, mats):
    tail = jnp.full((2, HD), lengths[0].astype(F32)).astype(BF)
    for y in range(NY):
        for m in range(4):
            start = (m * NY + y) * HD if m < 3 else y * HD
            source = qkv if m < 3 else out
            block = source[:, start : start + HD]
            for c in range(2):
                mats[2 * y + c, m, 0:30, :] = block
                mats[2 * y + c, m, 30:32, :] = tail


def norm_kernel(scalars, raw, own, gain, normed, mine):
    core = scalars[0]
    gain_rows = gain[...].T
    for u in range(2):
        picks = [raw[x, 2 * core + u] for x in range(4)]
        values = jnp.concatenate(picks, axis=0)
        normalize(values, gain_rows, normed, utterance(u))
    project(normed, own, 0, mine, 0)
    pl.when(core == 0)(lambda: project(normed, own, 1, mine, 1))


def attend_kernel(
    scalars, raw, normed, mine, own, other, partial, kept, rest, context
):
    core = scalars[0]
    xi, yi = scalars[1], scalars[2]
    for u in range(2):
        kept[:, utterance(u)] = raw[xi, 2 * core + u, yi]

    def attend_all(query, keys, values):
        for u in range(2):
            columns = utterance(u)
            context[:, columns] = attend(
                query[:, columns], keys[:, columns], values[:, columns], scalars[3 + u]
            )

    def out_from(high):
        for group in range(4):
            for b in range(4 * group, 4 * group + 4):
                partial[b] = matmul(high[b, 1], context[...]).astype(BF)

    def on_first():
        project(normed, other, 0, rest, 0)
        attend_all(mine.at[0], mine.at[1], rest.at[0])
        out_from(other)

    def on_second():
        project(normed, other, 0, rest, 0)
        project(normed, other, 1, rest, 1)
        attend_all(rest.at[0], rest.at[1], mine.at[0])
        out_from(own)

    pl.when(core == 0)(on_first)
    pl.when(core == 1)(on_second)


def stage_kernel(weights_hbm, staged, arrived):
    copy = pltpu.make_async_copy(weights_hbm.at[:, pl.ds(0, 3)], staged, arrived)
    copy.start()
    copy.wait()


def second_kernel(scalars, x1, weights, gain, rest, packed, normed, qkv):
    core = scalars[0]
    rows = []
    gain_rows = gain[...].T
    for u in range(2):
        normalize(x1[:, :, utterance(u)], gain_rows, normed, utterance(u))
    for index in range(3):
        project(normed, weights, index, qkv, index)
    for u in range(2):
        length = scalars[3 + u]
        columns = utterance(u)
        context = attend(qkv[0, :, columns], qkv[1, :, columns], qkv[2, :, columns], length)
        valid = lax.broadcasted_iota(jnp.int32, (128, HD), 0) < length
        total = jnp.where(valid, context.astype(F32).T, F32(0.0))
        pooled = jnp.sum(total, axis=0, keepdims=True) / length.astype(F32)
        rows.append(jnp.concatenate([pooled, rest[u : u + 1, :]], axis=1))
    mine = jnp.concatenate(rows, axis=0)
    first = jnp.where(core == 0, mine, F32(0.0))
    second = jnp.where(core == 1, mine, F32(0.0))
    block = jnp.concatenate([first, second], axis=0)
    for z in range(16):
        packed[z] = block


def cost(flops, moved):
    return pl.CostEstimate(flops=flops, bytes_accessed=moved, transcendentals=32768)


def run_regroup(lengths, qkv, out):
    return pl.pallas_call(
        regroup_kernel,
        out_shape=jax.ShapeDtypeStruct((2 * NY, 4, 32, HD), BF),
        in_specs=[SMEM, VMEM, VMEM],
        out_specs=VMEM,
        cost_estimate=cost(0, 400_000),
        name="regroup",
    )(lengths, qkv, out)


def run_norm(scalars, raw, own, gain):
    return pl.pallas_call(
        norm_kernel,
        out_shape=(
            jax.ShapeDtypeStruct((CHUNKS, HD, 256), BF),
            jax.ShapeDtypeStruct((2, HD, 256), BF),
        ),
        in_specs=[SMEM] + [VMEM] * 3,
        out_specs=(VMEM, VMEM),
        compiler_params=pltpu.CompilerParams(vmem_limit_bytes=20 << 20),
        cost_estimate=cost(400_000_000, 4_000_000),
        name="first_norm",
    )(scalars, raw, own, gain)


def run_attend(scalars, raw, normed, mine, own, other):
    return pl.pallas_call(
        attend_kernel,
        out_shape=(
            jax.ShapeDtypeStruct((CHUNKS, HD, 256), BF),
            jax.ShapeDtypeStruct((HD, 256), BF),
        ),
        in_specs=[SMEM] + [VMEM] * 5,
        out_specs=(VMEM, VMEM),
        scratch_shapes=[
            pltpu.VMEM((2, HD, 256), BF),
            pltpu.VMEM((HD, 256), BF),
        ],
        compiler_params=pltpu.CompilerParams(vmem_limit_bytes=20 << 20),
        cost_estimate=cost(600_000_000, 5_000_000),
        name="first_attend",
    )(scalars, raw, normed, mine, own, other)


def run_stage(weights):
    return pl.pallas_call(
        stage_kernel,
        out_shape=jax.ShapeDtypeStruct((CHUNKS, 3, HD, HD), BF),
        in_specs=[pl.BlockSpec(memory_space=pltpu.HBM)],
        out_specs=VMEM,
        scratch_shapes=[pltpu.SemaphoreType.DMA],
        compiler_params=pltpu.CompilerParams(vmem_limit_bytes=20 << 20),
        cost_estimate=cost(0, 3_000_000),
        name="stage",
    )(weights)


def run_second(scalars, x1, weights, gain, rest):
    return pl.pallas_call(
        second_kernel,
        out_shape=jax.ShapeDtypeStruct((16, 4, 2 * HD), F32),
        in_specs=[SMEM] + [VMEM] * 4,
        out_specs=VMEM,
        scratch_shapes=[
            pltpu.VMEM((CHUNKS, HD, 256), BF),
            pltpu.VMEM((3, HD, 256), BF),
        ],
        compiler_params=pltpu.CompilerParams(vmem_limit_bytes=20 << 20),
        cost_estimate=cost(1_000_000_000, 6_000_000),
        name="second_layer",
    )(scalars, x1, weights, gain, rest)


def body(frames, lengths, feature_proj, norm_gain, qkv_weight, out_weight, center, whitening):
    core = lax.axis_index("c")
    xi, yi = lax.axis_index("x"), lax.axis_index("y")
    chunk = xi * NY + yi

    projected = lax.dot_general(
        feature_proj, frames[0], (((0,), (1,)), ((), ())), preferred_element_type=F32
    )
    projected = projected.astype(BF).reshape(1, NY, HD, 128)
    projected = jnp.broadcast_to(projected, (16, NY, HD, 128))

    mats = run_regroup(lengths, qkv_weight[0], out_weight[0].T)
    regrouped = lax.all_to_all(mats, ("y", "c"), 0, 0).reshape(NY, 2, 4, 32, HD)
    gains = lax.all_gather(norm_gain[0], "c", axis=0)
    regrouped, gains, projected = lax.optimization_barrier((regrouped, gains, projected))
    plane_lengths = regrouped[:, 0, 0, 30, 0].astype(jnp.int32)
    my_lengths = lax.dynamic_slice_in_dim(plane_lengths, 2 * core, 2, 0)

    def shard(layer):
        rows = regrouped[:, layer, :, :30].transpose(1, 0, 2, 3).reshape(4, HD, HD)
        return jnp.concatenate([rows[:3].transpose(0, 2, 1), rows[3:]], axis=0)

    first_shard = lax.dynamic_slice_in_dim(shard(0), 2 * core, 2, 0)
    first_shard, second_shard, my_lengths = lax.optimization_barrier(
        (first_shard, shard(1), my_lengths)
    )
    second_weights = lax.all_gather(second_shard, "z", axis=0)
    own = lax.all_gather(first_shard, "z", axis=0)
    other = swap_cores(own)

    raw = lax.all_to_all(projected, ("x", "y"), 0, 0).reshape(4, NY, NY, HD, 128)

    scalars = jnp.concatenate([jnp.stack([core, xi, yi]).astype(jnp.int32), my_lengths])
    gains = gains.reshape(2, CHUNKS, HD)
    normed, mine = run_norm(scalars, raw, own, gains[0])
    partial, x0_own = run_attend(scalars, raw, normed, mine, own, other)
    white = whitening.T.reshape(16, CHUNKS, HD).transpose(1, 0, 2)
    x0_own, white = lax.optimization_barrier((x0_own, white))
    near = [(((y + 1 + c) % NY) * 2 + c, y * 2 + c) for y in range(NY) for c in range(2)]
    far = [(((y + 3) % NY) * 2 + 1, y * 2 + 1) for y in range(NY)]
    white_near = lax.ppermute(white, ("y", "c"), near)
    white_far = lax.ppermute(white, ("y", "c"), far)

    partial = lax.all_to_all(partial, ("x", "y"), 0, 0)
    attended = jnp.sum(partial.astype(F32), axis=0)
    x1_own = (x0_own.astype(F32) + attended).astype(BF)
    x1 = plane_gather(x1_own)

    valid = jnp.arange(128)[None, :] < my_lengths[:, None]
    share = valid.astype(F32) / my_lengths.astype(F32)[:, None]
    pooled_x1 = jnp.sum(x1_own.reshape(HD, 2, 128).astype(F32) * share, axis=2).T
    center_own = lax.dynamic_index_in_dim(center.reshape(CHUNKS, HD), chunk, 0, keepdims=False)
    staged = run_stage(second_weights)
    packed = run_second(scalars, x1, staged, gains[1], pooled_x1 - center_own)

    white_cols = jnp.stack(
        [jnp.where(core == 0, white, white_near), jnp.where(core == 0, white_near, white_far)]
    )
    out_white = jnp.einsum(
        "ybnc,bcr->ynr",
        white_cols,
        second_weights[:, 3].astype(F32),
        precision=lax.Precision.HIGHEST,
    )
    white_own = lax.dynamic_index_in_dim(white_cols, chunk, 1, keepdims=False)
    mixed = jnp.concatenate([out_white, white_own], axis=2)
    swapped = swap_cores(mixed)
    low = jnp.where(core == 0, mixed, swapped)
    high = jnp.where(core == 0, swapped, mixed)
    mixed = jnp.concatenate([low, high, low, high], axis=0)
    mixed = lax.dynamic_slice_in_dim(mixed, (NY - yi) % NY, NY, 0).reshape(64, 2 * HD)

    packed = lax.all_to_all(packed, "z", 0, 0).reshape(64, 2 * HD)
    part = jnp.einsum("tk,nk->nt", packed, mixed, precision=lax.Precision.HIGHEST)
    part = jnp.broadcast_to(part.reshape(NY, 1, 16, 64), (NY, 8, 16, 64)).reshape(32, 16, 64)
    part = lax.all_to_all(part, ("y", "c", "x"), 0, 0)
    return jnp.sum(part, axis=0).T


def solution(mesh):
    devices = mesh.devices.reshape(-1, NY, 2, 4)
    split = Mesh(devices, ("z", "y", "c", "x"))
    dp = ("z", "y")
    in_specs = (
        P(dp, None, None),
        P(dp),
        P(None, "x"),
        P("c", None),
        P("c", dp, "x"),
        P("c", "x", dp),
        P(),
        P(None, dp),
    )
    return jax.shard_map(
        body, mesh=split, in_specs=in_specs, out_specs=P(None, dp), check_vma=False
    )
```

```python
import jax
import jax.numpy as jnp
from jax import lax
from jax.experimental import pallas as pl
from jax.experimental.pallas import tpu as pltpu
from jax.sharding import Mesh, PartitionSpec as P

HD = 120
NY = 4
CHUNKS = 16
BF = jnp.bfloat16
F32 = jnp.float32
VMEM = pl.BlockSpec(memory_space=pltpu.VMEM)
SMEM = pl.BlockSpec(memory_space=pltpu.SMEM)


def plane_gather(block):
    count = lax.axis_size("x") * lax.axis_size("y")
    spread = jnp.broadcast_to(block[None], (count,) + block.shape)
    return lax.all_to_all(spread, ("x", "y"), 0, 0)


def swap_cores(value):
    return lax.ppermute(value, "c", [(0, 1), (1, 0)])


def matmul(left, right):
    return jnp.dot(left, right, preferred_element_type=F32)


def normalize(values, gain_rows, out_ref, columns):
    values = values.astype(F32)
    width = CHUNKS * HD
    mean = jnp.sum(jnp.sum(values, axis=0), axis=0, keepdims=True) / width
    centered = values - mean[None]
    var = jnp.sum(jnp.sum(centered * centered, axis=0), axis=0, keepdims=True) / width
    scale = lax.rsqrt(var + 1e-05)
    for b in range(CHUNKS):
        out_ref[b, :, columns] = (centered[b] * scale * gain_rows[:, b : b + 1]).astype(BF)


def project(normed_ref, weight_ref, index, out_ref, slot):
    total = jnp.zeros((HD, 256), F32)
    for b in range(CHUNKS):
        total += matmul(weight_ref[b, index], normed_ref[b])
    out_ref[slot] = total.astype(BF)


def attend(query, keys, values, length):
    keys = keys.astype(F32).T.astype(BF)
    scores = matmul(keys, query) / jnp.sqrt(F32(HD))
    place = lax.broadcasted_iota(jnp.int32, (128, 128), 0)
    scores = jnp.where(place < length, scores, F32(-1e30))
    top = jnp.max(scores, axis=0, keepdims=True)
    grown = jnp.exp(scores - top)
    probs = (grown / jnp.sum(grown, axis=0, keepdims=True)).astype(BF)
    return matmul(values, probs).astype(BF)


def utterance(u):
    return slice(u * 128, u * 128 + 128)


def regroup_kernel(lengths, qkv, out, mats):
    tail = jnp.broadcast_to(lengths[...].astype(F32), (2, HD)).astype(BF)
    for y in range(NY):
        for m in range(4):
            start = (m * NY + y) * HD if m < 3 else y * HD
            source = qkv if m < 3 else out
            block = source[:, start : start + HD]
            for c in range(2):
                mats[2 * y + c, m, 0:30, :] = block
                mats[2 * y + c, m, 30:32, :] = tail


def input_kernel(weights, frames, spread):
    projected = lax.dot_general(
        weights[...], frames[...], (((1,), (1,)), ((), ())), preferred_element_type=F32
    )
    for y in range(NY):
        block = projected[y * HD : y * HD + HD, :].astype(BF)
        for target in range(16):
            spread[target, y] = block


def norm_kernel(scalars, raw, own, gain, normed, mine):
    core = scalars[0]
    gain_rows = gain[...].T
    for u in range(2):
        picks = [raw[x, 2 * core + u] for x in range(4)]
        values = jnp.concatenate(picks, axis=0)
        normalize(values, gain_rows, normed, utterance(u))
    project(normed, own, 0, mine, 0)
    pl.when(core == 0)(lambda: project(normed, own, 1, mine, 1))


def attend_kernel(
    scalars, raw, normed, mine, own, other, partial, kept, rest, context
):
    core = scalars[0]
    xi, yi = scalars[1], scalars[2]
    for u in range(2):
        kept[:, utterance(u)] = raw[xi, 2 * core + u, yi]

    def attend_all(query, keys, values):
        for u in range(2):
            columns = utterance(u)
            context[:, columns] = attend(
                query[:, columns], keys[:, columns], values[:, columns], scalars[3 + u]
            )

    def out_from(high):
        for group in range(4):
            for b in range(4 * group, 4 * group + 4):
                partial[b] = matmul(high[b, 1], context[...]).astype(BF)

    def on_first():
        project(normed, other, 0, rest, 0)
        attend_all(mine.at[0], mine.at[1], rest.at[0])
        out_from(other)

    def on_second():
        project(normed, other, 0, rest, 0)
        project(normed, other, 1, rest, 1)
        attend_all(rest.at[0], rest.at[1], mine.at[0])
        out_from(own)

    pl.when(core == 0)(on_first)
    pl.when(core == 1)(on_second)


def stage_kernel(weights_hbm, staged, arrived):
    copy = pltpu.make_async_copy(weights_hbm.at[:, pl.ds(0, 3)], staged, arrived)
    copy.start()
    copy.wait()


def second_kernel(scalars, x1, weights, gain, rest, packed, normed, qkv):
    core = scalars[0]
    rows = []
    gain_rows = gain[...].T
    for u in range(2):
        normalize(x1[:, :, utterance(u)], gain_rows, normed, utterance(u))
    for index in range(3):
        project(normed, weights, index, qkv, index)
    for u in range(2):
        length = scalars[3 + u]
        columns = utterance(u)
        context = attend(qkv[0, :, columns], qkv[1, :, columns], qkv[2, :, columns], length)
        valid = lax.broadcasted_iota(jnp.int32, (128, HD), 0) < length
        total = jnp.where(valid, context.astype(F32).T, F32(0.0))
        pooled = jnp.sum(total, axis=0, keepdims=True) / length.astype(F32)
        rows.append(jnp.concatenate([pooled, rest[u : u + 1, :]], axis=1))
    mine = jnp.concatenate(rows, axis=0)
    first = jnp.where(core == 0, mine, F32(0.0))
    second = jnp.where(core == 1, mine, F32(0.0))
    block = jnp.concatenate([first, second], axis=0)
    for z in range(16):
        packed[z] = block


def cost(flops, moved):
    return pl.CostEstimate(flops=flops, bytes_accessed=moved, transcendentals=32768)


def run_regroup(lengths, qkv, out):
    return pl.pallas_call(
        regroup_kernel,
        out_shape=jax.ShapeDtypeStruct((2 * NY, 4, 32, HD), BF),
        in_specs=[VMEM, VMEM, VMEM],
        out_specs=VMEM,
        cost_estimate=cost(0, 400_000),
        name="regroup",
    )(lengths, qkv, out)


def run_input(weights, frames):
    return pl.pallas_call(
        input_kernel,
        out_shape=jax.ShapeDtypeStruct((16, NY, HD, 128), BF),
        in_specs=[VMEM, VMEM],
        out_specs=VMEM,
        compiler_params=pltpu.CompilerParams(vmem_limit_bytes=20 << 20),
        cost_estimate=cost(100_000_000, 3_000_000),
        name="layer_input",
    )(weights, frames)


def run_norm(scalars, raw, own, gain):
    return pl.pallas_call(
        norm_kernel,
        out_shape=(
            jax.ShapeDtypeStruct((CHUNKS, HD, 256), BF),
            jax.ShapeDtypeStruct((2, HD, 256), BF),
        ),
        in_specs=[SMEM] + [VMEM] * 3,
        out_specs=(VMEM, VMEM),
        compiler_params=pltpu.CompilerParams(vmem_limit_bytes=20 << 20),
        cost_estimate=cost(400_000_000, 4_000_000),
        name="first_norm",
    )(scalars, raw, own, gain)


def run_attend(scalars, raw, normed, mine, own, other):
    return pl.pallas_call(
        attend_kernel,
        out_shape=(
            jax.ShapeDtypeStruct((CHUNKS, HD, 256), BF),
            jax.ShapeDtypeStruct((HD, 256), BF),
        ),
        in_specs=[SMEM] + [VMEM] * 5,
        out_specs=(VMEM, VMEM),
        scratch_shapes=[
            pltpu.VMEM((2, HD, 256), BF),
            pltpu.VMEM((HD, 256), BF),
        ],
        compiler_params=pltpu.CompilerParams(vmem_limit_bytes=20 << 20),
        cost_estimate=cost(600_000_000, 5_000_000),
        name="first_attend",
    )(scalars, raw, normed, mine, own, other)


def run_stage(weights):
    return pl.pallas_call(
        stage_kernel,
        out_shape=jax.ShapeDtypeStruct((CHUNKS, 3, HD, HD), BF),
        in_specs=[pl.BlockSpec(memory_space=pltpu.HBM)],
        out_specs=VMEM,
        scratch_shapes=[pltpu.SemaphoreType.DMA],
        compiler_params=pltpu.CompilerParams(vmem_limit_bytes=20 << 20),
        cost_estimate=cost(0, 3_000_000),
        name="stage",
    )(weights)


def run_second(scalars, x1, weights, gain, rest):
    return pl.pallas_call(
        second_kernel,
        out_shape=jax.ShapeDtypeStruct((16, 4, 2 * HD), F32),
        in_specs=[SMEM] + [VMEM] * 4,
        out_specs=VMEM,
        scratch_shapes=[
            pltpu.VMEM((CHUNKS, HD, 256), BF),
            pltpu.VMEM((3, HD, 256), BF),
        ],
        compiler_params=pltpu.CompilerParams(vmem_limit_bytes=20 << 20),
        cost_estimate=cost(1_000_000_000, 6_000_000),
        name="second_layer",
    )(scalars, x1, weights, gain, rest)


def body(frames, lengths, feature_proj, norm_gain, qkv_weight, out_weight, center, whitening):
    core = lax.axis_index("c")
    xi, yi = lax.axis_index("x"), lax.axis_index("y")
    chunk = xi * NY + yi

    projected = run_input(feature_proj.T, frames[0])

    mats = run_regroup(lengths.reshape(1, 1), qkv_weight[0], out_weight[0].T)
    regrouped = lax.all_to_all(mats, ("y", "c"), 0, 0).reshape(NY, 2, 4, 32, HD)
    gains = lax.all_gather(norm_gain[0], "c", axis=0)
    regrouped, gains, projected = lax.optimization_barrier((regrouped, gains, projected))
    plane_lengths = jnp.max(regrouped[:, 0, 0, 30].astype(F32), axis=1).astype(jnp.int32)
    my_lengths = lax.dynamic_slice_in_dim(plane_lengths, 2 * core, 2, 0)

    def shard(layer):
        rows = regrouped[:, layer, :, :30].transpose(1, 0, 2, 3).reshape(4, HD, HD)
        return jnp.concatenate([rows[:3].transpose(0, 2, 1), rows[3:]], axis=0)

    first_shard = lax.dynamic_slice_in_dim(shard(0), 2 * core, 2, 0)
    first_shard, second_shard, my_lengths = lax.optimization_barrier(
        (first_shard, shard(1), my_lengths)
    )
    second_weights = lax.all_gather(second_shard, "z", axis=0)
    own = lax.all_gather(first_shard, "z", axis=0)
    other = swap_cores(own)

    raw = lax.all_to_all(projected, ("x", "y"), 0, 0).reshape(4, NY, NY, HD, 128)

    scalars = jnp.concatenate([jnp.stack([core, xi, yi]).astype(jnp.int32), my_lengths])
    gains = gains.reshape(2, CHUNKS, HD)
    normed, mine = run_norm(scalars, raw, own, gains[0])
    partial, x0_own = run_attend(scalars, raw, normed, mine, own, other)
    white = whitening.T.reshape(16, CHUNKS, HD).transpose(1, 0, 2)
    x0_own, white = lax.optimization_barrier((x0_own, white))
    near = [(((y + 1 + c) % NY) * 2 + c, y * 2 + c) for y in range(NY) for c in range(2)]
    far = [(((y + 3) % NY) * 2 + 1, y * 2 + 1) for y in range(NY)]
    white_near = lax.ppermute(white, ("y", "c"), near)
    white_far = lax.ppermute(white, ("y", "c"), far)

    partial = lax.all_to_all(partial, ("x", "y"), 0, 0)
    attended = jnp.sum(partial.astype(F32), axis=0)
    x1_own = (x0_own.astype(F32) + attended).astype(BF)
    x1 = plane_gather(x1_own)

    valid = jnp.arange(128)[None, :] < my_lengths[:, None]
    share = valid.astype(F32) / my_lengths.astype(F32)[:, None]
    pooled_x1 = jnp.sum(x1_own.reshape(HD, 2, 128).astype(F32) * share, axis=2).T
    center_own = lax.dynamic_index_in_dim(center.reshape(CHUNKS, HD), chunk, 0, keepdims=False)
    staged = run_stage(second_weights)
    packed = run_second(scalars, x1, staged, gains[1], pooled_x1 - center_own)

    white_cols = jnp.stack(
        [jnp.where(core == 0, white, white_near), jnp.where(core == 0, white_near, white_far)]
    )
    out_white = jnp.einsum(
        "ybnc,bcr->ynr",
        white_cols,
        second_weights[:, 3].astype(F32),
        precision=lax.Precision.HIGHEST,
    )
    white_own = lax.dynamic_index_in_dim(white_cols, chunk, 1, keepdims=False)
    mixed = jnp.concatenate([out_white, white_own], axis=2)
    swapped = swap_cores(mixed)
    low = jnp.where(core == 0, mixed, swapped)
    high = jnp.where(core == 0, swapped, mixed)
    mixed = jnp.concatenate([low, high, low, high], axis=0)
    mixed = lax.dynamic_slice_in_dim(mixed, (NY - yi) % NY, NY, 0).reshape(64, 2 * HD)

    packed = lax.all_to_all(packed, "z", 0, 0).reshape(64, 2 * HD)
    part = jnp.einsum("tk,nk->nt", packed, mixed, precision=lax.Precision.HIGHEST)
    part = jnp.pad(part, ((0, 0), (0, 64))).reshape(NY, 1, 16, 128)
    part = jnp.broadcast_to(part, (NY, 8, 16, 128)).reshape(32, 16, 128)
    part = lax.all_to_all(part, ("y", "c", "x"), 0, 0)
    return jnp.sum(part, axis=0)[:, :64].T


def solution(mesh):
    devices = mesh.devices.reshape(-1, NY, 2, 4)
    split = Mesh(devices, ("z", "y", "c", "x"))
    dp = ("z", "y")
    in_specs = (
        P(dp, None, None),
        P(dp),
        P(None, "x"),
        P("c", None),
        P("c", dp, "x"),
        P("c", "x", dp),
        P(),
        P(None, dp),
    )
    return jax.shard_map(
        body, mesh=split, in_specs=in_specs, out_specs=P(None, dp), check_vma=False
    )
```

```python
import jax
import jax.numpy as jnp
from jax import lax
from jax.experimental import pallas as pl
from jax.experimental.pallas import tpu as pltpu
from jax.sharding import Mesh, PartitionSpec as P

HD = 120
NY = 4
CHUNKS = 16
BF = jnp.bfloat16
F32 = jnp.float32
VMEM = pl.BlockSpec(memory_space=pltpu.VMEM)
SMEM = pl.BlockSpec(memory_space=pltpu.SMEM)


def plane_gather(block):
    count = lax.axis_size("x") * lax.axis_size("y")
    spread = jnp.broadcast_to(block[None], (count,) + block.shape)
    return lax.all_to_all(spread, ("x", "y"), 0, 0)


def pass_along(value, distance):
    count = lax.axis_size("z")
    pairs = []
    for z in range(count):
        for c in range(2):
            target = (z + (distance if c == 0 else -distance)) % count
            pairs.append((2 * z + c, 2 * target + c))
    return lax.ppermute(value, ("z", "c"), pairs)


def swap_cores(value):
    return lax.ppermute(value, "c", [(0, 1), (1, 0)])


def matmul(left, right):
    return jnp.dot(left, right, preferred_element_type=F32)


def normalize(values, gain_rows, out_ref, columns):
    values = values.astype(F32)
    width = CHUNKS * HD
    mean = jnp.sum(jnp.sum(values, axis=0), axis=0, keepdims=True) / width
    centered = values - mean[None]
    var = jnp.sum(jnp.sum(centered * centered, axis=0), axis=0, keepdims=True) / width
    scale = lax.rsqrt(var + 1e-05)
    for b in range(CHUNKS):
        out_ref[b, :, columns] = (centered[b] * scale * gain_rows[:, b : b + 1]).astype(BF)


def project(normed_ref, weight_ref, index, out_ref, slot):
    total = jnp.zeros((HD, 256), F32)
    for b in range(CHUNKS):
        total += matmul(weight_ref[b, index], normed_ref[b])
    out_ref[slot] = total.astype(BF)


def held(pieces, steps):
    return [(pieces[step % 3].at[step // 3], step) for step in steps]


OWN_STEPS = tuple(range(0, 8))
OTHER_STEPS = tuple(range(1, 9))
OWN_AT = 5
OTHER_AT = 14


def attend(query, keys, values, length):
    keys = keys.astype(F32).T.astype(BF)
    scores = matmul(keys, query) / jnp.sqrt(F32(HD))
    place = lax.broadcasted_iota(jnp.int32, (128, 128), 0)
    scores = jnp.where(place < length, scores, F32(-1e30))
    top = jnp.max(scores, axis=0, keepdims=True)
    grown = jnp.exp(scores - top)
    probs = (grown / jnp.sum(grown, axis=0, keepdims=True)).astype(BF)
    return matmul(values, probs).astype(BF)


def utterance(u):
    return slice(u * 128, u * 128 + 128)


def regroup_kernel(lengths, qkv, out, mats):
    tail = jnp.broadcast_to(lengths[...].astype(F32), (2, HD)).astype(BF)
    for y in range(NY):
        for m in range(4):
            start = (m * NY + y) * HD if m < 3 else y * HD
            source = qkv if m < 3 else out
            block = source[:, start : start + HD]
            for c in range(2):
                mats[2 * y + c, m, 0:30, :] = block
                mats[2 * y + c, m, 30:32, :] = tail


def input_kernel(weights, frames, spread):
    projected = lax.dot_general(
        weights[...], frames[...], (((1,), (1,)), ((), ())), preferred_element_type=F32
    )
    for y in range(NY):
        block = projected[y * HD : y * HD + HD, :].astype(BF)
        for target in range(16):
            spread[target, y] = block


def norm_kernel(scalars, raw, own0, own1, own2, gain, normed, sums):
    core = scalars[0]
    gain_rows = gain[...].T
    for u in range(2):
        picks = [raw[x, 2 * core + u] for x in range(4)]
        values = jnp.concatenate(picks, axis=0)
        normalize(values, gain_rows, normed, utterance(u))
    for index in range(3):
        total = jnp.zeros((HD, 256), F32)
        for piece, step in held((own0, own1, own2), OWN_STEPS):
            total += matmul(piece[index], normed[scalars[OWN_AT + step]])
        sums[index] = total


def attend_kernel(
    scalars, raw, normed, sums, own0, own1, own2, other0, other1, other2, partial, kept, qkv, context
):
    core = scalars[0]
    xi, yi = scalars[1], scalars[2]
    own = held((own0, own1, own2), OWN_STEPS)
    other = held((other0, other1, other2), OTHER_STEPS)
    for u in range(2):
        kept[:, utterance(u)] = raw[xi, 2 * core + u, yi]
    for index in range(3):
        total = sums[index]
        for piece, step in other:
            total += matmul(piece[index], normed[scalars[OTHER_AT + step]])
        qkv[index] = total.astype(BF)
    for u in range(2):
        columns = utterance(u)
        context[:, columns] = attend(
            qkv[0, :, columns], qkv[1, :, columns], qkv[2, :, columns], scalars[3 + u]
        )
    for piece, step in own:
        partial[scalars[OWN_AT + step]] = matmul(piece[3], context[...]).astype(BF)
    for piece, step in other:
        partial[scalars[OTHER_AT + step]] = matmul(piece[3], context[...]).astype(BF)


def stage_kernel(weights_hbm, staged, arrived):
    copy = pltpu.make_async_copy(weights_hbm.at[:, pl.ds(0, 3)], staged, arrived)
    copy.start()
    copy.wait()


def second_kernel(scalars, x1, weights, gain, rest, packed, normed, qkv):
    core = scalars[0]
    rows = []
    gain_rows = gain[...].T
    for u in range(2):
        normalize(x1[:, :, utterance(u)], gain_rows, normed, utterance(u))
    for index in range(3):
        project(normed, weights, index, qkv, index)
    for u in range(2):
        length = scalars[3 + u]
        columns = utterance(u)
        context = attend(qkv[0, :, columns], qkv[1, :, columns], qkv[2, :, columns], length)
        valid = lax.broadcasted_iota(jnp.int32, (128, HD), 0) < length
        total = jnp.where(valid, context.astype(F32).T, F32(0.0))
        pooled = jnp.sum(total, axis=0, keepdims=True) / length.astype(F32)
        rows.append(jnp.concatenate([pooled, rest[u : u + 1, :]], axis=1))
    mine = jnp.concatenate(rows, axis=0)
    first = jnp.where(core == 0, mine, F32(0.0))
    second = jnp.where(core == 1, mine, F32(0.0))
    block = jnp.concatenate([first, second], axis=0)
    for z in range(16):
        packed[z] = block


def cost(flops, moved):
    return pl.CostEstimate(flops=flops, bytes_accessed=moved, transcendentals=32768)


def run_regroup(lengths, qkv, out):
    return pl.pallas_call(
        regroup_kernel,
        out_shape=jax.ShapeDtypeStruct((2 * NY, 4, 32, HD), BF),
        in_specs=[VMEM, VMEM, VMEM],
        out_specs=VMEM,
        cost_estimate=cost(0, 400_000),
        name="regroup",
    )(lengths, qkv, out)


def run_input(weights, frames):
    return pl.pallas_call(
        input_kernel,
        out_shape=jax.ShapeDtypeStruct((16, NY, HD, 128), BF),
        in_specs=[VMEM, VMEM],
        out_specs=VMEM,
        compiler_params=pltpu.CompilerParams(vmem_limit_bytes=20 << 20),
        cost_estimate=cost(100_000_000, 3_000_000),
        name="layer_input",
    )(weights, frames)


def run_norm(scalars, raw, own, gain):
    return pl.pallas_call(
        norm_kernel,
        out_shape=(
            jax.ShapeDtypeStruct((CHUNKS, HD, 256), BF),
            jax.ShapeDtypeStruct((3, HD, 256), F32),
        ),
        in_specs=[SMEM] + [VMEM] * 5,
        out_specs=(VMEM, VMEM),
        compiler_params=pltpu.CompilerParams(vmem_limit_bytes=20 << 20),
        cost_estimate=cost(400_000_000, 4_000_000),
        name="first_norm",
    )(scalars, raw, *own, gain)


def run_attend(scalars, raw, normed, sums, own, other):
    return pl.pallas_call(
        attend_kernel,
        out_shape=(
            jax.ShapeDtypeStruct((CHUNKS, HD, 256), BF),
            jax.ShapeDtypeStruct((HD, 256), BF),
        ),
        in_specs=[SMEM] + [VMEM] * 9,
        out_specs=(VMEM, VMEM),
        scratch_shapes=[
            pltpu.VMEM((3, HD, 256), BF),
            pltpu.VMEM((HD, 256), BF),
        ],
        compiler_params=pltpu.CompilerParams(vmem_limit_bytes=20 << 20),
        cost_estimate=cost(600_000_000, 5_000_000),
        name="first_attend",
    )(scalars, raw, normed, sums, *own, *other)


def run_stage(weights):
    return pl.pallas_call(
        stage_kernel,
        out_shape=jax.ShapeDtypeStruct((CHUNKS, 3, HD, HD), BF),
        in_specs=[pl.BlockSpec(memory_space=pltpu.HBM)],
        out_specs=VMEM,
        scratch_shapes=[pltpu.SemaphoreType.DMA],
        compiler_params=pltpu.CompilerParams(vmem_limit_bytes=20 << 20),
        cost_estimate=cost(0, 3_000_000),
        name="stage",
    )(weights)


def run_second(scalars, x1, weights, gain, rest):
    return pl.pallas_call(
        second_kernel,
        out_shape=jax.ShapeDtypeStruct((16, 4, 2 * HD), F32),
        in_specs=[SMEM] + [VMEM] * 4,
        out_specs=VMEM,
        scratch_shapes=[
            pltpu.VMEM((CHUNKS, HD, 256), BF),
            pltpu.VMEM((3, HD, 256), BF),
        ],
        compiler_params=pltpu.CompilerParams(vmem_limit_bytes=20 << 20),
        cost_estimate=cost(1_000_000_000, 6_000_000),
        name="second_layer",
    )(scalars, x1, weights, gain, rest)


def body(frames, lengths, feature_proj, norm_gain, qkv_weight, out_weight, center, whitening):
    core = lax.axis_index("c")
    xi, yi = lax.axis_index("x"), lax.axis_index("y")
    chunk = xi * NY + yi

    projected = run_input(feature_proj.T, frames[0])

    mats = run_regroup(lengths.reshape(1, 1), qkv_weight[0], out_weight[0].T)
    regrouped = lax.all_to_all(mats, ("y", "c"), 0, 0).reshape(NY, 2, 4, 32, HD)
    gains = lax.all_gather(norm_gain[0], "c", axis=0)
    regrouped, gains, projected = lax.optimization_barrier((regrouped, gains, projected))
    plane_lengths = jnp.max(regrouped[:, 0, 0, 30].astype(F32), axis=1).astype(jnp.int32)
    my_lengths = lax.dynamic_slice_in_dim(plane_lengths, 2 * core, 2, 0)

    def shard(layer):
        rows = regrouped[:, layer, :, :30].transpose(1, 0, 2, 3).reshape(4, HD, HD)
        return jnp.concatenate([rows[:3].transpose(0, 2, 1), rows[3:]], axis=0)

    first_shard, second_shard, my_lengths = lax.optimization_barrier(
        (shard(0), shard(1), my_lengths)
    )
    second_weights = lax.all_gather(second_shard, "z", axis=0)
    by_three = jnp.stack(
        [first_shard, pass_along(first_shard, 3), pass_along(first_shard, 6)]
    )
    own = (by_three, pass_along(by_three, 1), pass_along(by_three, 2))
    other = tuple(swap_cores(piece) for piece in own)
    sign = 2 * core - 1
    steps = jnp.arange(9, dtype=jnp.int32)
    zi = lax.axis_index("z")
    own_at = (zi + sign * steps) % CHUNKS
    other_at = (zi - sign * steps) % CHUNKS

    raw = lax.all_to_all(projected, ("x", "y"), 0, 0).reshape(4, NY, NY, HD, 128)

    scalars = jnp.concatenate(
        [jnp.stack([core, xi, yi]).astype(jnp.int32), my_lengths, own_at, other_at]
    )
    gains = gains.reshape(2, CHUNKS, HD)
    normed, sums = run_norm(scalars, raw, own, gains[0])
    partial, x0_own = run_attend(scalars, raw, normed, sums, own, other)
    white = whitening.T.reshape(16, CHUNKS, HD).transpose(1, 0, 2)
    x0_own, white = lax.optimization_barrier((x0_own, white))
    near = [(((y + 1 + c) % NY) * 2 + c, y * 2 + c) for y in range(NY) for c in range(2)]
    far = [(((y + 3) % NY) * 2 + 1, y * 2 + 1) for y in range(NY)]
    white_near = lax.ppermute(white, ("y", "c"), near)
    white_far = lax.ppermute(white, ("y", "c"), far)

    partial = lax.all_to_all(partial, ("x", "y"), 0, 0)
    attended = jnp.sum(partial.astype(F32), axis=0)
    x1_own = (x0_own.astype(F32) + attended).astype(BF)
    x1 = plane_gather(x1_own)

    valid = jnp.arange(128)[None, :] < my_lengths[:, None]
    share = valid.astype(F32) / my_lengths.astype(F32)[:, None]
    pooled_x1 = jnp.sum(x1_own.reshape(HD, 2, 128).astype(F32) * share, axis=2).T
    center_own = lax.dynamic_index_in_dim(center.reshape(CHUNKS, HD), chunk, 0, keepdims=False)
    staged = run_stage(second_weights)
    packed = run_second(scalars, x1, staged, gains[1], pooled_x1 - center_own)

    white_cols = jnp.stack(
        [jnp.where(core == 0, white, white_near), jnp.where(core == 0, white_near, white_far)]
    )
    out_white = jnp.einsum(
        "ybnc,bcr->ynr",
        white_cols,
        second_weights[:, 3].astype(F32),
        precision=lax.Precision.HIGHEST,
    )
    white_own = lax.dynamic_index_in_dim(white_cols, chunk, 1, keepdims=False)
    mixed = jnp.concatenate([out_white, white_own], axis=2)
    swapped = swap_cores(mixed)
    low = jnp.where(core == 0, mixed, swapped)
    high = jnp.where(core == 0, swapped, mixed)
    mixed = jnp.concatenate([low, high, low, high], axis=0)
    mixed = lax.dynamic_slice_in_dim(mixed, (NY - yi) % NY, NY, 0).reshape(64, 2 * HD)

    packed = lax.all_to_all(packed, "z", 0, 0).reshape(64, 2 * HD)
    part = jnp.einsum("tk,nk->nt", packed, mixed, precision=lax.Precision.HIGHEST)
    part = jnp.pad(part, ((0, 0), (0, 64))).reshape(NY, 1, 16, 128)
    part = jnp.broadcast_to(part, (NY, 8, 16, 128)).reshape(32, 16, 128)
    part = lax.all_to_all(part, ("y", "c", "x"), 0, 0)
    return jnp.sum(part, axis=0)[:, :64].T


def solution(mesh):
    devices = mesh.devices.reshape(-1, NY, 2, 4)
    split = Mesh(devices, ("z", "y", "c", "x"))
    dp = ("z", "y")
    in_specs = (
        P(dp, None, None),
        P(dp),
        P(None, "x"),
        P("c", None),
        P("c", dp, "x"),
        P("c", "x", dp),
        P(),
        P(None, dp),
    )
    return jax.shard_map(
        body, mesh=split, in_specs=in_specs, out_specs=P(None, dp), check_vma=False
    )
```

```python
import jax
import jax.numpy as jnp
from jax import lax
from jax.experimental import pallas as pl
from jax.experimental.pallas import tpu as pltpu
from jax.sharding import Mesh, PartitionSpec as P

HD = 120
NY = 4
CHUNKS = 16
BF = jnp.bfloat16
F32 = jnp.float32
VMEM = pl.BlockSpec(memory_space=pltpu.VMEM)
SMEM = pl.BlockSpec(memory_space=pltpu.SMEM)


def swap_cores(value):
    return lax.ppermute(value, "c", [(0, 1), (1, 0)])


def matmul(left, right):
    return jnp.dot(left, right, preferred_element_type=F32)


def normalize(values, gain_rows, out_ref, columns):
    values = values.astype(F32)
    width = CHUNKS * HD
    mean = jnp.sum(jnp.sum(values, axis=0), axis=0, keepdims=True) / width
    centered = values - mean[None]
    var = jnp.sum(jnp.sum(centered * centered, axis=0), axis=0, keepdims=True) / width
    scale = lax.rsqrt(var + 1e-05)
    for b in range(CHUNKS):
        out_ref[b, :, columns] = (centered[b] * scale * gain_rows[:, b : b + 1]).astype(BF)


def project(normed_ref, weight_ref, index, out_ref, slot):
    total = jnp.zeros((HD, 256), F32)
    for b in range(CHUNKS):
        total += matmul(weight_ref[b, index], normed_ref[b])
    out_ref[slot] = total.astype(BF)


def attend(query, keys, values, length):
    keys = keys.astype(F32).T.astype(BF)
    scores = matmul(keys, query) / jnp.sqrt(F32(HD))
    place = lax.broadcasted_iota(jnp.int32, (128, 128), 0)
    scores = jnp.where(place < length, scores, F32(-1e30))
    top = jnp.max(scores, axis=0, keepdims=True)
    grown = jnp.exp(scores - top)
    probs = (grown / jnp.sum(grown, axis=0, keepdims=True)).astype(BF)
    return matmul(values, probs).astype(BF)


def utterance(u):
    return slice(u * 128, u * 128 + 128)


def regroup_kernel(lengths, qkv, out, mats):
    tail = jnp.broadcast_to(lengths[...].astype(F32), (2, HD)).astype(BF)
    for y in range(NY):
        for m in range(4):
            start = (m * NY + y) * HD if m < 3 else y * HD
            source = qkv if m < 3 else out
            block = source[:, start : start + HD]
            for c in range(2):
                mats[2 * y + c, m, 0:30, :] = block
                mats[2 * y + c, m, 30:32, :] = tail


def input_kernel(weights, frames, spread):
    projected = lax.dot_general(
        weights[...], frames[...], (((1,), (1,)), ((), ())), preferred_element_type=F32
    )
    for y in range(NY):
        block = projected[y * HD : y * HD + HD, :].astype(BF)
        for target in range(16):
            spread[target, y] = block


def norm_kernel(scalars, raw, own, gain, normed, mine):
    core = scalars[0]
    gain_rows = gain[...].T
    for u in range(2):
        picks = [raw[x, 2 * core + u] for x in range(4)]
        values = jnp.concatenate(picks, axis=0)
        normalize(values, gain_rows, normed, utterance(u))
    project(normed, own, 0, mine, 0)
    pl.when(core == 0)(lambda: project(normed, own, 1, mine, 1))


def attend_kernel(
    scalars, raw, normed, mine, own, other, partial_hbm, kept, rest, context, partial, sent
):
    core = scalars[0]
    xi, yi = scalars[1], scalars[2]
    for u in range(2):
        kept[:, utterance(u)] = raw[xi, 2 * core + u, yi]

    def attend_all(query, keys, values):
        for u in range(2):
            columns = utterance(u)
            context[:, columns] = attend(
                query[:, columns], keys[:, columns], values[:, columns], scalars[3 + u]
            )

    def out_from(high):
        copies = []
        for group in range(4):
            chunks = pl.ds(4 * group, 4)
            for b in range(4 * group, 4 * group + 4):
                partial[b] = matmul(high[b, 1], context[...]).astype(BF)
            copies.append(
                pltpu.make_async_copy(partial.at[chunks], partial_hbm.at[chunks], sent.at[group])
            )
            copies[-1].start()
        for copy in copies:
            copy.wait()

    def on_first():
        project(normed, other, 0, rest, 0)
        attend_all(mine.at[0], mine.at[1], rest.at[0])
        out_from(other)

    def on_second():
        project(normed, other, 0, rest, 0)
        project(normed, other, 1, rest, 1)
        attend_all(rest.at[0], rest.at[1], mine.at[0])
        out_from(own)

    pl.when(core == 0)(on_first)
    pl.when(core == 1)(on_second)


def combine_kernel(partial, kept, spread, result, sent):
    total = partial[0].astype(F32)
    for head in range(1, CHUNKS):
        total += partial[head].astype(F32)
    result[...] = (kept[...].astype(F32) + total).astype(BF)
    copies = [
        pltpu.make_async_copy(result, spread.at[target], sent.at[target])
        for target in range(CHUNKS)
    ]
    for copy in copies:
        copy.start()
    for copy in copies:
        copy.wait()


def stage_kernel(weights_hbm, staged, arrived):
    copy = pltpu.make_async_copy(weights_hbm.at[:, pl.ds(0, 3)], staged, arrived)
    copy.start()
    copy.wait()


def second_kernel(scalars, x1, weights, gain, rest, packed, normed, qkv):
    core = scalars[0]
    rows = []
    gain_rows = gain[...].T
    for u in range(2):
        normalize(x1[:, :, utterance(u)], gain_rows, normed, utterance(u))
    for index in range(3):
        project(normed, weights, index, qkv, index)
    for u in range(2):
        length = scalars[3 + u]
        columns = utterance(u)
        context = attend(qkv[0, :, columns], qkv[1, :, columns], qkv[2, :, columns], length)
        valid = lax.broadcasted_iota(jnp.int32, (128, HD), 0) < length
        total = jnp.where(valid, context.astype(F32).T, F32(0.0))
        pooled = jnp.sum(total, axis=0, keepdims=True) / length.astype(F32)
        rows.append(jnp.concatenate([pooled, rest[u : u + 1, :]], axis=1))
    mine = jnp.concatenate(rows, axis=0)
    first = jnp.where(core == 0, mine, F32(0.0))
    second = jnp.where(core == 1, mine, F32(0.0))
    block = jnp.concatenate([first, second], axis=0)
    for z in range(16):
        packed[z] = block


def cost(flops, moved):
    return pl.CostEstimate(flops=flops, bytes_accessed=moved, transcendentals=32768)


def run_regroup(lengths, qkv, out):
    return pl.pallas_call(
        regroup_kernel,
        out_shape=jax.ShapeDtypeStruct((2 * NY, 4, 32, HD), BF),
        in_specs=[VMEM, VMEM, VMEM],
        out_specs=VMEM,
        cost_estimate=cost(0, 400_000),
        name="regroup",
    )(lengths, qkv, out)


def run_input(weights, frames):
    return pl.pallas_call(
        input_kernel,
        out_shape=jax.ShapeDtypeStruct((16, NY, HD, 128), BF),
        in_specs=[VMEM, VMEM],
        out_specs=VMEM,
        compiler_params=pltpu.CompilerParams(vmem_limit_bytes=20 << 20),
        cost_estimate=cost(100_000_000, 3_000_000),
        name="layer_input",
    )(weights, frames)


def run_norm(scalars, raw, own, gain):
    return pl.pallas_call(
        norm_kernel,
        out_shape=(
            jax.ShapeDtypeStruct((CHUNKS, HD, 256), BF),
            jax.ShapeDtypeStruct((2, HD, 256), BF),
        ),
        in_specs=[SMEM] + [VMEM] * 3,
        out_specs=(VMEM, VMEM),
        compiler_params=pltpu.CompilerParams(vmem_limit_bytes=20 << 20),
        cost_estimate=cost(400_000_000, 4_000_000),
        name="first_norm",
    )(scalars, raw, own, gain)


def run_attend(scalars, raw, normed, mine, own, other):
    return pl.pallas_call(
        attend_kernel,
        out_shape=(
            pltpu.HBM((CHUNKS, HD, 256), BF),
            jax.ShapeDtypeStruct((HD, 256), BF),
        ),
        in_specs=[SMEM] + [VMEM] * 5,
        out_specs=(pl.BlockSpec(memory_space=pltpu.HBM), VMEM),
        scratch_shapes=[
            pltpu.VMEM((2, HD, 256), BF),
            pltpu.VMEM((HD, 256), BF),
            pltpu.VMEM((CHUNKS, HD, 256), BF),
            pltpu.SemaphoreType.DMA((4,)),
        ],
        compiler_params=pltpu.CompilerParams(vmem_limit_bytes=20 << 20),
        cost_estimate=cost(600_000_000, 5_000_000),
        name="first_attend",
    )(scalars, raw, normed, mine, own, other)


def run_combine(partial, kept):
    return pl.pallas_call(
        combine_kernel,
        out_shape=(
            pltpu.HBM((CHUNKS, HD, 256), BF),
            jax.ShapeDtypeStruct((HD, 256), BF),
        ),
        in_specs=[VMEM, VMEM],
        out_specs=(pl.BlockSpec(memory_space=pltpu.HBM), VMEM),
        scratch_shapes=[pltpu.SemaphoreType.DMA((CHUNKS,))],
        compiler_params=pltpu.CompilerParams(vmem_limit_bytes=20 << 20),
        cost_estimate=cost(1_000_000, 2_000_000),
        name="combine",
    )(partial, kept)


def run_stage(weights):
    return pl.pallas_call(
        stage_kernel,
        out_shape=jax.ShapeDtypeStruct((CHUNKS, 3, HD, HD), BF),
        in_specs=[pl.BlockSpec(memory_space=pltpu.HBM)],
        out_specs=VMEM,
        scratch_shapes=[pltpu.SemaphoreType.DMA],
        compiler_params=pltpu.CompilerParams(vmem_limit_bytes=20 << 20),
        cost_estimate=cost(0, 3_000_000),
        name="stage",
    )(weights)


def run_second(scalars, x1, weights, gain, rest):
    return pl.pallas_call(
        second_kernel,
        out_shape=jax.ShapeDtypeStruct((16, 4, 2 * HD), F32),
        in_specs=[SMEM] + [VMEM] * 4,
        out_specs=VMEM,
        scratch_shapes=[
            pltpu.VMEM((CHUNKS, HD, 256), BF),
            pltpu.VMEM((3, HD, 256), BF),
        ],
        compiler_params=pltpu.CompilerParams(vmem_limit_bytes=20 << 20),
        cost_estimate=cost(1_000_000_000, 6_000_000),
        name="second_layer",
    )(scalars, x1, weights, gain, rest)


def body(frames, lengths, feature_proj, norm_gain, qkv_weight, out_weight, center, whitening):
    core = lax.axis_index("c")
    xi, yi = lax.axis_index("x"), lax.axis_index("y")
    chunk = xi * NY + yi

    projected = run_input(feature_proj.T, frames[0])

    mats = run_regroup(lengths.reshape(1, 1), qkv_weight[0], out_weight[0].T)
    regrouped = lax.all_to_all(mats, ("y", "c"), 0, 0).reshape(NY, 2, 4, 32, HD)
    gains = lax.all_gather(norm_gain[0], "c", axis=0)
    regrouped, gains, projected = lax.optimization_barrier((regrouped, gains, projected))
    plane_lengths = jnp.max(regrouped[:, 0, 0, 30].astype(F32), axis=1).astype(jnp.int32)
    my_lengths = lax.dynamic_slice_in_dim(plane_lengths, 2 * core, 2, 0)

    def shard(layer):
        rows = regrouped[:, layer, :, :30].transpose(1, 0, 2, 3).reshape(4, HD, HD)
        return jnp.concatenate([rows[:3].transpose(0, 2, 1), rows[3:]], axis=0)

    first_shard = lax.dynamic_slice_in_dim(shard(0), 2 * core, 2, 0)
    first_shard, second_shard, my_lengths = lax.optimization_barrier(
        (first_shard, shard(1), my_lengths)
    )
    second_weights = lax.all_gather(second_shard, "z", axis=0)
    own = lax.all_gather(first_shard, "z", axis=0)
    other = swap_cores(own)

    raw = lax.all_to_all(projected, ("x", "y"), 0, 0).reshape(4, NY, NY, HD, 128)

    scalars = jnp.concatenate([jnp.stack([core, xi, yi]).astype(jnp.int32), my_lengths])
    gains = gains.reshape(2, CHUNKS, HD)
    normed, mine = run_norm(scalars, raw, own, gains[0])
    partial, x0_own = run_attend(scalars, raw, normed, mine, own, other)
    white = whitening.T.reshape(16, CHUNKS, HD).transpose(1, 0, 2)
    x0_own, white = lax.optimization_barrier((x0_own, white))
    near = [(((y + 1 + c) % NY) * 2 + c, y * 2 + c) for y in range(NY) for c in range(2)]
    far = [(((y + 3) % NY) * 2 + 1, y * 2 + 1) for y in range(NY)]
    white_near = lax.ppermute(white, ("y", "c"), near)
    white_far = lax.ppermute(white, ("y", "c"), far)

    partial = lax.all_to_all(partial, ("x", "y"), 0, 0)
    spread, x1_own = run_combine(partial, x0_own)
    x1 = lax.all_to_all(spread, ("x", "y"), 0, 0)

    valid = jnp.arange(128)[None, :] < my_lengths[:, None]
    share = valid.astype(F32) / my_lengths.astype(F32)[:, None]
    pooled_x1 = jnp.sum(x1_own.reshape(HD, 2, 128).astype(F32) * share, axis=2).T
    center_own = lax.dynamic_index_in_dim(center.reshape(CHUNKS, HD), chunk, 0, keepdims=False)
    staged = run_stage(second_weights)
    packed = run_second(scalars, x1, staged, gains[1], pooled_x1 - center_own)

    white_cols = jnp.stack(
        [jnp.where(core == 0, white, white_near), jnp.where(core == 0, white_near, white_far)]
    )
    out_white = jnp.einsum(
        "ybnc,bcr->ynr",
        white_cols,
        second_weights[:, 3].astype(F32),
        precision=lax.Precision.HIGHEST,
    )
    white_own = lax.dynamic_index_in_dim(white_cols, chunk, 1, keepdims=False)
    mixed = jnp.concatenate([out_white, white_own], axis=2)
    swapped = swap_cores(mixed)
    low = jnp.where(core == 0, mixed, swapped)
    high = jnp.where(core == 0, swapped, mixed)
    mixed = jnp.concatenate([low, high, low, high], axis=0)
    mixed = lax.dynamic_slice_in_dim(mixed, (NY - yi) % NY, NY, 0).reshape(64, 2 * HD)

    packed = lax.all_to_all(packed, "z", 0, 0).reshape(64, 2 * HD)
    part = jnp.einsum("tk,nk->nt", packed, mixed, precision=lax.Precision.HIGHEST)
    part = part.reshape(NY, 1, 2, 8, 64)
    part = jnp.concatenate([part[:, :, 0], part[:, :, 1]], axis=3)
    part = jnp.broadcast_to(part, (NY, 8, 8, 128)).reshape(32, 8, 128)
    part = lax.all_to_all(part, ("y", "c", "x"), 0, 0)
    total = jnp.sum(part, axis=0)
    return jnp.concatenate([total[:, :64], total[:, 64:]], axis=0).T


def solution(mesh):
    devices = mesh.devices.reshape(-1, NY, 2, 4)
    split = Mesh(devices, ("z", "y", "c", "x"))
    dp = ("z", "y")
    in_specs = (
        P(dp, None, None),
        P(dp),
        P(None, "x"),
        P("c", None),
        P("c", dp, "x"),
        P("c", "x", dp),
        P(),
        P(None, dp),
    )
    return jax.shard_map(
        body, mesh=split, in_specs=in_specs, out_specs=P(None, dp), check_vma=False
    )
```

```python
import jax
import jax.numpy as jnp
from jax import lax
from jax.experimental import pallas as pl
from jax.experimental.pallas import tpu as pltpu
from jax.sharding import Mesh, PartitionSpec as P

HD = 120
NY = 4
CHUNKS = 16
BF = jnp.bfloat16
F32 = jnp.float32
VMEM = pl.BlockSpec(memory_space=pltpu.VMEM)
SMEM = pl.BlockSpec(memory_space=pltpu.SMEM)


def swap_cores(value):
    return lax.ppermute(value, "c", [(0, 1), (1, 0)])


def matmul(left, right):
    return jnp.dot(left, right, preferred_element_type=F32)


def normalize(values, gain_rows, out_ref, columns):
    values = values.astype(F32)
    width = CHUNKS * HD
    mean = jnp.sum(jnp.sum(values, axis=0), axis=0, keepdims=True) / width
    centered = values - mean[None]
    var = jnp.sum(jnp.sum(centered * centered, axis=0), axis=0, keepdims=True) / width
    scale = lax.rsqrt(var + 1e-05)
    for b in range(CHUNKS):
        out_ref[b, :, columns] = (centered[b] * scale * gain_rows[:, b : b + 1]).astype(BF)


def project(normed_ref, weight_ref, index, out_ref, slot):
    total = jnp.zeros((HD, 256), F32)
    for b in range(CHUNKS):
        total += matmul(weight_ref[b, index], normed_ref[b])
    out_ref[slot] = total.astype(BF)


def attend(query, keys, values, length):
    keys = keys.astype(F32).T.astype(BF)
    scores = matmul(keys, query) / jnp.sqrt(F32(HD))
    place = lax.broadcasted_iota(jnp.int32, (128, 128), 0)
    scores = jnp.where(place < length, scores, F32(-1e30))
    top = jnp.max(scores, axis=0, keepdims=True)
    grown = jnp.exp(scores - top)
    probs = (grown / jnp.sum(grown, axis=0, keepdims=True)).astype(BF)
    return matmul(values, probs).astype(BF)


def utterance(u):
    return slice(u * 128, u * 128 + 128)


def regroup_kernel(lengths, qkv, out, mats_hbm, mats, sent):
    tail = jnp.broadcast_to(lengths[...].astype(F32), (2, HD)).astype(BF)
    copies = []
    for y in range(NY):
        for m in range(4):
            start = (m * NY + y) * HD if m < 3 else y * HD
            source = qkv if m < 3 else out
            mats[y, m, 0:30, :] = source[:, start : start + HD]
            mats[y, m, 30:32, :] = tail
        for c in range(2):
            target = 2 * y + c
            copies.append(
                pltpu.make_async_copy(mats.at[y], mats_hbm.at[target], sent.at[target])
            )
            copies[-1].start()
    for copy in copies:
        copy.wait()


def input_kernel(weights_hbm, frames_hbm, spread, weights, frames, blocks, arrived, sent):
    fetches = [
        pltpu.make_async_copy(weights_hbm, weights, arrived.at[0]),
        pltpu.make_async_copy(frames_hbm, frames, arrived.at[1]),
    ]
    for fetch in fetches:
        fetch.start()
    for fetch in fetches:
        fetch.wait()
    projected = lax.dot_general(
        weights[...], frames[...], (((1,), (1,)), ((), ())), preferred_element_type=F32
    )
    for y in range(NY):
        blocks[y] = projected[y * HD : y * HD + HD, :].astype(BF)
    copies = [
        pltpu.make_async_copy(blocks, spread.at[target], sent.at[target]) for target in range(16)
    ]
    for copy in copies:
        copy.start()
    for copy in copies:
        copy.wait()


def norm_kernel(scalars, raw, own, gain, normed, mine):
    core = scalars[0]
    gain_rows = gain[...].T
    for u in range(2):
        picks = [raw[x, 2 * core + u] for x in range(4)]
        values = jnp.concatenate(picks, axis=0)
        normalize(values, gain_rows, normed, utterance(u))
    project(normed, own, 0, mine, 0)
    pl.when(core == 0)(lambda: project(normed, own, 1, mine, 1))


def attend_kernel(
    scalars, raw, normed, mine, own, other, partial_hbm, kept, rest, context, partial, sent
):
    core = scalars[0]
    xi, yi = scalars[1], scalars[2]
    for u in range(2):
        kept[:, utterance(u)] = raw[xi, 2 * core + u, yi]

    def attend_all(query, keys, values):
        for u in range(2):
            columns = utterance(u)
            context[:, columns] = attend(
                query[:, columns], keys[:, columns], values[:, columns], scalars[3 + u]
            )

    def out_from(high):
        copies = []
        for group in range(4):
            chunks = pl.ds(4 * group, 4)
            for b in range(4 * group, 4 * group + 4):
                partial[b] = matmul(high[b, 1], context[...]).astype(BF)
            copies.append(
                pltpu.make_async_copy(partial.at[chunks], partial_hbm.at[chunks], sent.at[group])
            )
            copies[-1].start()
        for copy in copies:
            copy.wait()

    def on_first():
        project(normed, other, 0, rest, 0)
        attend_all(mine.at[0], mine.at[1], rest.at[0])
        out_from(other)

    def on_second():
        project(normed, other, 0, rest, 0)
        project(normed, other, 1, rest, 1)
        attend_all(rest.at[0], rest.at[1], mine.at[0])
        out_from(own)

    pl.when(core == 0)(on_first)
    pl.when(core == 1)(on_second)


def combine_kernel(partial, kept, spread, result, sent):
    total = partial[0].astype(F32)
    for head in range(1, CHUNKS):
        total += partial[head].astype(F32)
    result[...] = (kept[...].astype(F32) + total).astype(BF)
    copies = [
        pltpu.make_async_copy(result, spread.at[target], sent.at[target])
        for target in range(CHUNKS)
    ]
    for copy in copies:
        copy.start()
    for copy in copies:
        copy.wait()


def stage_kernel(weights_hbm, staged, arrived):
    copy = pltpu.make_async_copy(weights_hbm.at[:, pl.ds(0, 3)], staged, arrived)
    copy.start()
    copy.wait()


def second_kernel(scalars, x1, weights, gain, rest, packed, normed, qkv):
    core = scalars[0]
    rows = []
    gain_rows = gain[...].T
    for u in range(2):
        normalize(x1[:, :, utterance(u)], gain_rows, normed, utterance(u))
    for index in range(3):
        project(normed, weights, index, qkv, index)
    for u in range(2):
        length = scalars[3 + u]
        columns = utterance(u)
        context = attend(qkv[0, :, columns], qkv[1, :, columns], qkv[2, :, columns], length)
        valid = lax.broadcasted_iota(jnp.int32, (128, HD), 0) < length
        total = jnp.where(valid, context.astype(F32).T, F32(0.0))
        pooled = jnp.sum(total, axis=0, keepdims=True) / length.astype(F32)
        rows.append(jnp.concatenate([pooled, rest[u : u + 1, :]], axis=1))
    mine = jnp.concatenate(rows, axis=0)
    first = jnp.where(core == 0, mine, F32(0.0))
    second = jnp.where(core == 1, mine, F32(0.0))
    block = jnp.concatenate([first, second], axis=0)
    for z in range(16):
        packed[z] = block


def cost(flops, moved):
    return pl.CostEstimate(flops=flops, bytes_accessed=moved, transcendentals=32768)


def run_regroup(lengths, qkv, out):
    return pl.pallas_call(
        regroup_kernel,
        out_shape=pltpu.HBM((2 * NY, 4, 32, HD), BF),
        in_specs=[VMEM, VMEM, VMEM],
        out_specs=pl.BlockSpec(memory_space=pltpu.HBM),
        scratch_shapes=[
            pltpu.VMEM((NY, 4, 32, HD), BF),
            pltpu.SemaphoreType.DMA((2 * NY,)),
        ],
        cost_estimate=cost(0, 400_000),
        name="regroup",
    )(lengths, qkv, out)


def run_input(weights, frames):
    hbm = pl.BlockSpec(memory_space=pltpu.HBM)
    return pl.pallas_call(
        input_kernel,
        out_shape=pltpu.HBM((16, NY, HD, 128), BF),
        in_specs=[hbm, hbm],
        out_specs=hbm,
        scratch_shapes=[
            pltpu.VMEM(weights.shape, BF),
            pltpu.VMEM(frames.shape, BF),
            pltpu.VMEM((NY, HD, 128), BF),
            pltpu.SemaphoreType.DMA((2,)),
            pltpu.SemaphoreType.DMA((16,)),
        ],
        compiler_params=pltpu.CompilerParams(vmem_limit_bytes=20 << 20),
        cost_estimate=cost(100_000_000, 3_000_000),
        name="layer_input",
    )(
        pltpu.with_memory_space_constraint(weights, pltpu.HBM),
        pltpu.with_memory_space_constraint(frames, pltpu.HBM),
    )


def run_norm(scalars, raw, own, gain):
    return pl.pallas_call(
        norm_kernel,
        out_shape=(
            jax.ShapeDtypeStruct((CHUNKS, HD, 256), BF),
            jax.ShapeDtypeStruct((2, HD, 256), BF),
        ),
        in_specs=[SMEM] + [VMEM] * 3,
        out_specs=(VMEM, VMEM),
        compiler_params=pltpu.CompilerParams(vmem_limit_bytes=20 << 20),
        cost_estimate=cost(400_000_000, 4_000_000),
        name="first_norm",
    )(scalars, raw, own, gain)


def run_attend(scalars, raw, normed, mine, own, other):
    return pl.pallas_call(
        attend_kernel,
        out_shape=(
            pltpu.HBM((CHUNKS, HD, 256), BF),
            jax.ShapeDtypeStruct((HD, 256), BF),
        ),
        in_specs=[SMEM] + [VMEM] * 5,
        out_specs=(pl.BlockSpec(memory_space=pltpu.HBM), VMEM),
        scratch_shapes=[
            pltpu.VMEM((2, HD, 256), BF),
            pltpu.VMEM((HD, 256), BF),
            pltpu.VMEM((CHUNKS, HD, 256), BF),
            pltpu.SemaphoreType.DMA((4,)),
        ],
        compiler_params=pltpu.CompilerParams(vmem_limit_bytes=20 << 20),
        cost_estimate=cost(600_000_000, 5_000_000),
        name="first_attend",
    )(scalars, raw, normed, mine, own, other)


def run_combine(partial, kept):
    return pl.pallas_call(
        combine_kernel,
        out_shape=(
            pltpu.HBM((CHUNKS, HD, 256), BF),
            jax.ShapeDtypeStruct((HD, 256), BF),
        ),
        in_specs=[VMEM, VMEM],
        out_specs=(pl.BlockSpec(memory_space=pltpu.HBM), VMEM),
        scratch_shapes=[pltpu.SemaphoreType.DMA((CHUNKS,))],
        compiler_params=pltpu.CompilerParams(vmem_limit_bytes=20 << 20),
        cost_estimate=cost(1_000_000, 2_000_000),
        name="combine",
    )(partial, kept)


def run_stage(weights):
    return pl.pallas_call(
        stage_kernel,
        out_shape=jax.ShapeDtypeStruct((CHUNKS, 3, HD, HD), BF),
        in_specs=[pl.BlockSpec(memory_space=pltpu.HBM)],
        out_specs=VMEM,
        scratch_shapes=[pltpu.SemaphoreType.DMA],
        compiler_params=pltpu.CompilerParams(vmem_limit_bytes=20 << 20),
        cost_estimate=cost(0, 3_000_000),
        name="stage",
    )(weights)


def run_second(scalars, x1, weights, gain, rest):
    return pl.pallas_call(
        second_kernel,
        out_shape=jax.ShapeDtypeStruct((16, 4, 2 * HD), F32),
        in_specs=[SMEM] + [VMEM] * 4,
        out_specs=VMEM,
        scratch_shapes=[
            pltpu.VMEM((CHUNKS, HD, 256), BF),
            pltpu.VMEM((3, HD, 256), BF),
        ],
        compiler_params=pltpu.CompilerParams(vmem_limit_bytes=20 << 20),
        cost_estimate=cost(1_000_000_000, 6_000_000),
        name="second_layer",
    )(scalars, x1, weights, gain, rest)


def body(frames, lengths, feature_proj, norm_gain, qkv_weight, out_weight, center, whitening):
    core = lax.axis_index("c")
    xi, yi = lax.axis_index("x"), lax.axis_index("y")
    chunk = xi * NY + yi

    projected = run_input(feature_proj.T, frames[0])

    mats = run_regroup(lengths.reshape(1, 1), qkv_weight[0], out_weight[0].T)
    regrouped = lax.all_to_all(mats, ("y", "c"), 0, 0).reshape(NY, 2, 4, 32, HD)
    gains = lax.all_gather(norm_gain[0], "c", axis=0)
    regrouped, gains, projected = lax.optimization_barrier((regrouped, gains, projected))
    plane_lengths = jnp.max(regrouped[:, 0, 0, 30].astype(F32), axis=1).astype(jnp.int32)
    my_lengths = lax.dynamic_slice_in_dim(plane_lengths, 2 * core, 2, 0)

    def shard(layer):
        rows = regrouped[:, layer, :, :30].transpose(1, 0, 2, 3).reshape(4, HD, HD)
        return jnp.concatenate([rows[:3].transpose(0, 2, 1), rows[3:]], axis=0)

    first_shard = lax.dynamic_slice_in_dim(shard(0), 2 * core, 2, 0)
    first_shard, second_shard, my_lengths = lax.optimization_barrier(
        (first_shard, shard(1), my_lengths)
    )
    second_weights = lax.all_gather(second_shard, "z", axis=0)
    own = lax.all_gather(first_shard, "z", axis=0)
    other = swap_cores(own)

    raw = lax.all_to_all(projected, ("x", "y"), 0, 0).reshape(4, NY, NY, HD, 128)

    scalars = jnp.concatenate([jnp.stack([core, xi, yi]).astype(jnp.int32), my_lengths])
    gains = gains.reshape(2, CHUNKS, HD)
    normed, mine = run_norm(scalars, raw, own, gains[0])
    partial, x0_own = run_attend(scalars, raw, normed, mine, own, other)
    white = whitening.T.reshape(16, CHUNKS, HD).transpose(1, 0, 2)
    x0_own, white = lax.optimization_barrier((x0_own, white))
    near = [(((y + 1 + c) % NY) * 2 + c, y * 2 + c) for y in range(NY) for c in range(2)]
    far = [(((y + 3) % NY) * 2 + 1, y * 2 + 1) for y in range(NY)]
    white_near = lax.ppermute(white, ("y", "c"), near)
    white_far = lax.ppermute(white, ("y", "c"), far)

    partial = lax.all_to_all(partial, ("x", "y"), 0, 0)
    spread, x1_own = run_combine(partial, x0_own)
    x1 = lax.all_to_all(spread, ("x", "y"), 0, 0)

    valid = jnp.arange(128)[None, :] < my_lengths[:, None]
    share = valid.astype(F32) / my_lengths.astype(F32)[:, None]
    pooled_x1 = jnp.sum(x1_own.reshape(HD, 2, 128).astype(F32) * share, axis=2).T
    center_own = lax.dynamic_index_in_dim(center.reshape(CHUNKS, HD), chunk, 0, keepdims=False)
    staged = run_stage(second_weights)
    packed = run_second(scalars, x1, staged, gains[1], pooled_x1 - center_own)

    white_cols = jnp.stack(
        [jnp.where(core == 0, white, white_near), jnp.where(core == 0, white_near, white_far)]
    )
    out_white = jnp.einsum(
        "ybnc,bcr->ynr",
        white_cols,
        second_weights[:, 3].astype(F32),
        precision=lax.Precision.HIGHEST,
    )
    white_own = lax.dynamic_index_in_dim(white_cols, chunk, 1, keepdims=False)
    mixed = jnp.concatenate([out_white, white_own], axis=2)
    swapped = swap_cores(mixed)
    low = jnp.where(core == 0, mixed, swapped)
    high = jnp.where(core == 0, swapped, mixed)
    mixed = jnp.concatenate([low, high, low, high], axis=0)
    mixed = lax.dynamic_slice_in_dim(mixed, (NY - yi) % NY, NY, 0).reshape(64, 2 * HD)

    packed = lax.all_to_all(packed, "z", 0, 0).reshape(64, 2 * HD)
    part = jnp.einsum("tk,nk->nt", packed, mixed, precision=lax.Precision.HIGHEST)
    part = part.reshape(NY, 1, 2, 8, 64)
    part = jnp.concatenate([part[:, :, 0], part[:, :, 1]], axis=3)
    part = jnp.broadcast_to(part, (NY, 8, 8, 128)).reshape(32, 8, 128)
    part = lax.all_to_all(part, ("y", "c", "x"), 0, 0)
    total = jnp.sum(part, axis=0)
    return jnp.concatenate([total[:, :64], total[:, 64:]], axis=0).T


def solution(mesh):
    devices = mesh.devices.reshape(-1, NY, 2, 4)
    split = Mesh(devices, ("z", "y", "c", "x"))
    dp = ("z", "y")
    in_specs = (
        P(dp, None, None),
        P(dp),
        P(None, "x"),
        P("c", None),
        P("c", dp, "x"),
        P("c", "x", dp),
        P(),
        P(None, dp),
    )
    return jax.shard_map(
        body, mesh=split, in_specs=in_specs, out_specs=P(None, dp), check_vma=False
    )
```

```python
import jax
import jax.numpy as jnp
from jax import lax
from jax.experimental import pallas as pl
from jax.experimental.pallas import tpu as pltpu
from jax.sharding import Mesh, PartitionSpec as P

HD = 120
NY = 4
CHUNKS = 16
BF = jnp.bfloat16
F32 = jnp.float32
VMEM = pl.BlockSpec(memory_space=pltpu.VMEM)
SMEM = pl.BlockSpec(memory_space=pltpu.SMEM)


def swap_cores(value):
    return lax.ppermute(value, "c", [(0, 1), (1, 0)])


def matmul(left, right):
    return jnp.dot(left, right, preferred_element_type=F32)


def normalize(values, gain_rows, out_ref, columns):
    values = values.astype(F32)
    width = CHUNKS * HD
    mean = jnp.sum(jnp.sum(values, axis=0), axis=0, keepdims=True) / width
    centered = values - mean[None]
    var = jnp.sum(jnp.sum(centered * centered, axis=0), axis=0, keepdims=True) / width
    scale = lax.rsqrt(var + 1e-05)
    for b in range(CHUNKS):
        out_ref[b, :, columns] = (centered[b] * scale * gain_rows[:, b : b + 1]).astype(BF)


def project(normed_ref, weight_ref, index, out_ref, slot):
    total = jnp.zeros((HD, 256), F32)
    for b in range(CHUNKS):
        total += matmul(weight_ref[b, index], normed_ref[b])
    out_ref[slot] = total.astype(BF)


def attend(query, keys, values, length):
    keys = keys.astype(F32).T.astype(BF)
    scores = matmul(keys, query) / jnp.sqrt(F32(HD))
    place = lax.broadcasted_iota(jnp.int32, (128, 128), 0)
    scores = jnp.where(place < length, scores, F32(-1e30))
    top = jnp.max(scores, axis=0, keepdims=True)
    grown = jnp.exp(scores - top)
    probs = (grown / jnp.sum(grown, axis=0, keepdims=True)).astype(BF)
    return matmul(values, probs).astype(BF)


def utterance(u):
    return slice(u * 128, u * 128 + 128)


def regroup_kernel(lengths, qkv, out, mats_hbm, mats, sent):
    tail = jnp.broadcast_to(lengths[...].astype(F32), (2, HD)).astype(BF)
    copies = []
    for y in range(NY):
        for m in range(4):
            start = (m * NY + y) * HD if m < 3 else y * HD
            source = qkv if m < 3 else out
            mats[y, m, 0:30, :] = source[:, start : start + HD]
            mats[y, m, 30:32, :] = tail
        for c in range(2):
            target = 2 * y + c
            copies.append(
                pltpu.make_async_copy(mats.at[y], mats_hbm.at[target], sent.at[target])
            )
            copies[-1].start()
    for copy in copies:
        copy.wait()


def input_kernel(weights_hbm, frames_hbm, spread, weights, frames, blocks, arrived, sent):
    fetches = [
        pltpu.make_async_copy(weights_hbm, weights, arrived.at[0]),
        pltpu.make_async_copy(frames_hbm, frames, arrived.at[1]),
    ]
    for fetch in fetches:
        fetch.start()
    for fetch in fetches:
        fetch.wait()
    projected = lax.dot_general(
        weights[...], frames[...], (((1,), (1,)), ((), ())), preferred_element_type=F32
    )
    for y in range(NY):
        blocks[y] = projected[y * HD : y * HD + HD, :].astype(BF)
    copies = [
        pltpu.make_async_copy(blocks, spread.at[target], sent.at[target]) for target in range(16)
    ]
    for copy in copies:
        copy.start()
    for copy in copies:
        copy.wait()


def norm_kernel(scalars, raw, own, gain, normed, mine):
    core = scalars[0]
    gain_rows = gain[...].T
    for u in range(2):
        picks = [raw[x, 2 * core + u] for x in range(4)]
        values = jnp.concatenate(picks, axis=0)
        normalize(values, gain_rows, normed, utterance(u))
    project(normed, own, 0, mine, 0)
    pl.when(core == 0)(lambda: project(normed, own, 1, mine, 1))


def attend_kernel(
    scalars, raw, normed, mine, own, other, partial_hbm, kept, rest, context, partial, sent
):
    core = scalars[0]
    xi, yi = scalars[1], scalars[2]
    for u in range(2):
        kept[:, utterance(u)] = raw[xi, 2 * core + u, yi]

    def attend_all(query, keys, values):
        for u in range(2):
            columns = utterance(u)
            context[:, columns] = attend(
                query[:, columns], keys[:, columns], values[:, columns], scalars[3 + u]
            )

    def out_from(high):
        copies = []
        for group in range(4):
            chunks = pl.ds(4 * group, 4)
            for b in range(4 * group, 4 * group + 4):
                partial[b] = matmul(high[b, 1], context[...]).astype(BF)
            copies.append(
                pltpu.make_async_copy(partial.at[chunks], partial_hbm.at[chunks], sent.at[group])
            )
            copies[-1].start()
        for copy in copies:
            copy.wait()

    def on_first():
        project(normed, other, 0, rest, 0)
        attend_all(mine.at[0], mine.at[1], rest.at[0])
        out_from(other)

    def on_second():
        project(normed, other, 0, rest, 0)
        project(normed, other, 1, rest, 1)
        attend_all(rest.at[0], rest.at[1], mine.at[0])
        out_from(own)

    pl.when(core == 0)(on_first)
    pl.when(core == 1)(on_second)


def combine_kernel(partial, kept, spread, result, sent):
    total = partial[0].astype(F32)
    for head in range(1, CHUNKS):
        total += partial[head].astype(F32)
    result[...] = (kept[...].astype(F32) + total).astype(BF)
    copies = [
        pltpu.make_async_copy(result, spread.at[target], sent.at[target])
        for target in range(CHUNKS)
    ]
    for copy in copies:
        copy.start()
    for copy in copies:
        copy.wait()


def stage_kernel(weights_hbm, staged, arrived):
    copy = pltpu.make_async_copy(weights_hbm.at[:, pl.ds(0, 3)], staged, arrived)
    copy.start()
    copy.wait()


def second_kernel(scalars, x1, weights, gain, rest, packed, normed, qkv):
    rows = []
    gain_rows = gain[...].T
    for u in range(2):
        normalize(x1[:, :, utterance(u)], gain_rows, normed, utterance(u))
    for index in range(3):
        project(normed, weights, index, qkv, index)
    for u in range(2):
        length = scalars[3 + u]
        columns = utterance(u)
        context = attend(qkv[0, :, columns], qkv[1, :, columns], qkv[2, :, columns], length)
        valid = lax.broadcasted_iota(jnp.int32, (128, HD), 0) < length
        total = jnp.where(valid, context.astype(F32).T, F32(0.0))
        pooled = jnp.sum(total, axis=0, keepdims=True) / length.astype(F32)
        rows.append(jnp.concatenate([pooled, rest[u : u + 1, :]], axis=1))
    mine = jnp.concatenate(rows, axis=0)
    for target in range(32):
        packed[target] = mine


def cost(flops, moved):
    return pl.CostEstimate(flops=flops, bytes_accessed=moved, transcendentals=32768)


def run_regroup(lengths, qkv, out):
    return pl.pallas_call(
        regroup_kernel,
        out_shape=pltpu.HBM((2 * NY, 4, 32, HD), BF),
        in_specs=[VMEM, VMEM, VMEM],
        out_specs=pl.BlockSpec(memory_space=pltpu.HBM),
        scratch_shapes=[
            pltpu.VMEM((NY, 4, 32, HD), BF),
            pltpu.SemaphoreType.DMA((2 * NY,)),
        ],
        cost_estimate=cost(0, 400_000),
        name="regroup",
    )(lengths, qkv, out)


def run_input(weights, frames):
    hbm = pl.BlockSpec(memory_space=pltpu.HBM)
    return pl.pallas_call(
        input_kernel,
        out_shape=pltpu.HBM((16, NY, HD, 128), BF),
        in_specs=[hbm, hbm],
        out_specs=hbm,
        scratch_shapes=[
            pltpu.VMEM(weights.shape, BF),
            pltpu.VMEM(frames.shape, BF),
            pltpu.VMEM((NY, HD, 128), BF),
            pltpu.SemaphoreType.DMA((2,)),
            pltpu.SemaphoreType.DMA((16,)),
        ],
        compiler_params=pltpu.CompilerParams(vmem_limit_bytes=20 << 20),
        cost_estimate=cost(100_000_000, 3_000_000),
        name="layer_input",
    )(
        pltpu.with_memory_space_constraint(weights, pltpu.HBM),
        pltpu.with_memory_space_constraint(frames, pltpu.HBM),
    )


def run_norm(scalars, raw, own, gain):
    return pl.pallas_call(
        norm_kernel,
        out_shape=(
            jax.ShapeDtypeStruct((CHUNKS, HD, 256), BF),
            jax.ShapeDtypeStruct((2, HD, 256), BF),
        ),
        in_specs=[SMEM] + [VMEM] * 3,
        out_specs=(VMEM, VMEM),
        compiler_params=pltpu.CompilerParams(vmem_limit_bytes=20 << 20),
        cost_estimate=cost(400_000_000, 4_000_000),
        name="first_norm",
    )(scalars, raw, own, gain)


def run_attend(scalars, raw, normed, mine, own, other):
    return pl.pallas_call(
        attend_kernel,
        out_shape=(
            pltpu.HBM((CHUNKS, HD, 256), BF),
            jax.ShapeDtypeStruct((HD, 256), BF),
        ),
        in_specs=[SMEM] + [VMEM] * 5,
        out_specs=(pl.BlockSpec(memory_space=pltpu.HBM), VMEM),
        scratch_shapes=[
            pltpu.VMEM((2, HD, 256), BF),
            pltpu.VMEM((HD, 256), BF),
            pltpu.VMEM((CHUNKS, HD, 256), BF),
            pltpu.SemaphoreType.DMA((4,)),
        ],
        compiler_params=pltpu.CompilerParams(vmem_limit_bytes=20 << 20),
        cost_estimate=cost(600_000_000, 5_000_000),
        name="first_attend",
    )(scalars, raw, normed, mine, own, other)


def run_combine(partial, kept):
    return pl.pallas_call(
        combine_kernel,
        out_shape=(
            pltpu.HBM((CHUNKS, HD, 256), BF),
            jax.ShapeDtypeStruct((HD, 256), BF),
        ),
        in_specs=[VMEM, VMEM],
        out_specs=(pl.BlockSpec(memory_space=pltpu.HBM), VMEM),
        scratch_shapes=[pltpu.SemaphoreType.DMA((CHUNKS,))],
        compiler_params=pltpu.CompilerParams(vmem_limit_bytes=20 << 20),
        cost_estimate=cost(1_000_000, 2_000_000),
        name="combine",
    )(partial, kept)


def run_stage(weights):
    return pl.pallas_call(
        stage_kernel,
        out_shape=jax.ShapeDtypeStruct((CHUNKS, 3, HD, HD), BF),
        in_specs=[pl.BlockSpec(memory_space=pltpu.HBM)],
        out_specs=VMEM,
        scratch_shapes=[pltpu.SemaphoreType.DMA],
        compiler_params=pltpu.CompilerParams(vmem_limit_bytes=20 << 20),
        cost_estimate=cost(0, 3_000_000),
        name="stage",
    )(weights)


def run_second(scalars, x1, weights, gain, rest):
    return pl.pallas_call(
        second_kernel,
        out_shape=jax.ShapeDtypeStruct((32, 2, 2 * HD), F32),
        in_specs=[SMEM] + [VMEM] * 4,
        out_specs=VMEM,
        scratch_shapes=[
            pltpu.VMEM((CHUNKS, HD, 256), BF),
            pltpu.VMEM((3, HD, 256), BF),
        ],
        compiler_params=pltpu.CompilerParams(vmem_limit_bytes=20 << 20),
        cost_estimate=cost(1_000_000_000, 6_000_000),
        name="second_layer",
    )(scalars, x1, weights, gain, rest)


def body(frames, lengths, feature_proj, norm_gain, qkv_weight, out_weight, center, whitening):
    core = lax.axis_index("c")
    xi, yi = lax.axis_index("x"), lax.axis_index("y")
    chunk = xi * NY + yi

    projected = run_input(feature_proj.T, frames[0])

    mats = run_regroup(lengths.reshape(1, 1), qkv_weight[0], out_weight[0].T)
    regrouped = lax.all_to_all(mats, ("y", "c"), 0, 0).reshape(NY, 2, 4, 32, HD)
    gains = lax.all_gather(norm_gain[0], "c", axis=0)
    regrouped, gains, projected = lax.optimization_barrier((regrouped, gains, projected))
    plane_lengths = jnp.max(regrouped[:, 0, 0, 30].astype(F32), axis=1).astype(jnp.int32)
    my_lengths = lax.dynamic_slice_in_dim(plane_lengths, 2 * core, 2, 0)

    def shard(layer):
        rows = regrouped[:, layer, :, :30].transpose(1, 0, 2, 3).reshape(4, HD, HD)
        return jnp.concatenate([rows[:3].transpose(0, 2, 1), rows[3:]], axis=0)

    first_shard = lax.dynamic_slice_in_dim(shard(0), 2 * core, 2, 0)
    first_shard, second_shard, my_lengths = lax.optimization_barrier(
        (first_shard, shard(1), my_lengths)
    )
    second_weights = lax.all_gather(second_shard, "z", axis=0)
    own = lax.all_gather(first_shard, "z", axis=0)
    other = swap_cores(own)

    raw = lax.all_to_all(projected, ("x", "y"), 0, 0).reshape(4, NY, NY, HD, 128)

    scalars = jnp.concatenate([jnp.stack([core, xi, yi]).astype(jnp.int32), my_lengths])
    gains = gains.reshape(2, CHUNKS, HD)
    normed, mine = run_norm(scalars, raw, own, gains[0])
    partial, x0_own = run_attend(scalars, raw, normed, mine, own, other)
    white = whitening.T.reshape(16, CHUNKS, HD).transpose(1, 0, 2)
    x0_own, white = lax.optimization_barrier((x0_own, white))
    near = [(((y + 1 + c) % NY) * 2 + c, y * 2 + c) for y in range(NY) for c in range(2)]
    far = [(((y + 3) % NY) * 2 + 1, y * 2 + 1) for y in range(NY)]
    white_near = lax.ppermute(white, ("y", "c"), near)
    white_far = lax.ppermute(white, ("y", "c"), far)

    partial = lax.all_to_all(partial, ("x", "y"), 0, 0)
    spread, x1_own = run_combine(partial, x0_own)
    x1 = lax.all_to_all(spread, ("x", "y"), 0, 0)

    valid = jnp.arange(128)[None, :] < my_lengths[:, None]
    share = valid.astype(F32) / my_lengths.astype(F32)[:, None]
    pooled_x1 = jnp.sum(x1_own.reshape(HD, 2, 128).astype(F32) * share, axis=2).T
    center_own = lax.dynamic_index_in_dim(center.reshape(CHUNKS, HD), chunk, 0, keepdims=False)
    staged = run_stage(second_weights)
    packed = run_second(scalars, x1, staged, gains[1], pooled_x1 - center_own)

    white_cols = jnp.stack(
        [jnp.where(core == 0, white, white_near), jnp.where(core == 0, white_near, white_far)]
    )
    out_white = jnp.einsum(
        "ybnc,bcr->ynr",
        white_cols,
        second_weights[:, 3].astype(F32),
        precision=lax.Precision.HIGHEST,
    )
    white_own = lax.dynamic_index_in_dim(white_cols, chunk, 1, keepdims=False)
    mixed = jnp.concatenate([out_white, white_own], axis=2)
    swapped = swap_cores(mixed)
    low = jnp.where(core == 0, mixed, swapped)
    high = jnp.where(core == 0, swapped, mixed)
    mixed = jnp.concatenate([low, high, low, high], axis=0)
    mixed = lax.dynamic_slice_in_dim(mixed, (NY - yi) % NY, NY, 0).reshape(64, 2 * HD)

    packed = lax.all_to_all(packed, ("z", "c"), 0, 0).reshape(64, 2 * HD)
    part = jnp.einsum("tk,nk->nt", packed, mixed, precision=lax.Precision.HIGHEST)
    part = part.reshape(NY, 1, 2, 8, 64)
    part = jnp.concatenate([part[:, :, 0], part[:, :, 1]], axis=3)
    part = jnp.broadcast_to(part, (NY, 4, 8, 128)).reshape(16, 8, 128)
    part = lax.all_to_all(part, ("y", "x"), 0, 0)
    total = jnp.sum(part, axis=0)
    return jnp.concatenate([total[:, :64], total[:, 64:]], axis=0).T


def solution(mesh):
    devices = mesh.devices.reshape(-1, NY, 2, 4)
    split = Mesh(devices, ("z", "y", "c", "x"))
    dp = ("z", "y")
    in_specs = (
        P(dp, None, None),
        P(dp),
        P(None, "x"),
        P("c", None),
        P("c", dp, "x"),
        P("c", "x", dp),
        P(),
        P(None, dp),
    )
    return jax.shard_map(
        body, mesh=split, in_specs=in_specs, out_specs=P(None, dp), check_vma=False
    )
```

```python
import jax
import jax.numpy as jnp
from jax import lax
from jax.experimental import pallas as pl
from jax.experimental.pallas import tpu as pltpu
from jax.sharding import Mesh, PartitionSpec as P

HD = 120
NY = 4
CHUNKS = 16
BF = jnp.bfloat16
F32 = jnp.float32
VMEM = pl.BlockSpec(memory_space=pltpu.VMEM)
SMEM = pl.BlockSpec(memory_space=pltpu.SMEM)


def swap_cores(value):
    return lax.ppermute(value, "c", [(0, 1), (1, 0)])


def matmul(left, right):
    return jnp.dot(left, right, preferred_element_type=F32)


def normalize(values, gain_rows, out_ref, columns):
    values = values.astype(F32)
    width = CHUNKS * HD
    mean = jnp.sum(jnp.sum(values, axis=0), axis=0, keepdims=True) / width
    centered = values - mean[None]
    var = jnp.sum(jnp.sum(centered * centered, axis=0), axis=0, keepdims=True) / width
    scale = lax.rsqrt(var + 1e-05)
    for b in range(CHUNKS):
        out_ref[b, :, columns] = (centered[b] * scale * gain_rows[:, b : b + 1]).astype(BF)


def project(normed_ref, weight_ref, index, out_ref, slot):
    total = jnp.zeros((HD, 256), F32)
    for b in range(CHUNKS):
        total += matmul(weight_ref[b, index], normed_ref[b])
    out_ref[slot] = total.astype(BF)


def attend(query, keys, values, length):
    keys = keys.astype(F32).T.astype(BF)
    scores = matmul(keys, query) / jnp.sqrt(F32(HD))
    place = lax.broadcasted_iota(jnp.int32, (128, 128), 0)
    scores = jnp.where(place < length, scores, F32(-1e30))
    top = jnp.max(scores, axis=0, keepdims=True)
    grown = jnp.exp(scores - top)
    probs = (grown / jnp.sum(grown, axis=0, keepdims=True)).astype(BF)
    return matmul(values, probs).astype(BF)


def utterance(u):
    return slice(u * 128, u * 128 + 128)


def regroup_kernel(lengths, qkv, out, mats_hbm, mats, sent):
    tail = jnp.broadcast_to(lengths[...].astype(F32), (2, HD)).astype(BF)
    copies = []
    for y in range(NY):
        for m in range(4):
            start = (m * NY + y) * HD if m < 3 else y * HD
            source = qkv if m < 3 else out
            mats[y, m, 0:30, :] = source[:, start : start + HD]
            mats[y, m, 30:32, :] = tail
        for c in range(2):
            target = 2 * y + c
            copies.append(
                pltpu.make_async_copy(mats.at[y], mats_hbm.at[target], sent.at[target])
            )
            copies[-1].start()
    for copy in copies:
        copy.wait()


def input_kernel(weights_hbm, frames_hbm, spread, weights, frames, blocks, arrived, sent):
    fetches = [
        pltpu.make_async_copy(weights_hbm, weights, arrived.at[0]),
        pltpu.make_async_copy(frames_hbm, frames, arrived.at[1]),
    ]
    for fetch in fetches:
        fetch.start()
    for fetch in fetches:
        fetch.wait()
    projected = lax.dot_general(
        weights[...], frames[...], (((1,), (1,)), ((), ())), preferred_element_type=F32
    )
    for y in range(NY):
        blocks[y] = projected[y * HD : y * HD + HD, :].astype(BF)
    copies = [
        pltpu.make_async_copy(blocks, spread.at[target], sent.at[target]) for target in range(16)
    ]
    for copy in copies:
        copy.start()
    for copy in copies:
        copy.wait()


def norm_kernel(scalars, raw, own, gain, normed, mine):
    core = scalars[0]
    gain_rows = gain[...].T
    for u in range(2):
        picks = [raw[2 * core + u, x] for x in range(4)]
        values = jnp.concatenate(picks, axis=0)
        normalize(values, gain_rows, normed, utterance(u))
    project(normed, own, 0, mine, 0)
    pl.when(core == 0)(lambda: project(normed, own, 1, mine, 1))


def attend_kernel(
    scalars, raw, normed, mine, own, other, partial_hbm, kept, rest, context, partial, sent
):
    core = scalars[0]
    major, minor = scalars[1], scalars[2]
    for u in range(2):
        kept[:, utterance(u)] = raw[2 * core + u, major, minor]

    def attend_all(query, keys, values):
        for u in range(2):
            columns = utterance(u)
            context[:, columns] = attend(
                query[:, columns], keys[:, columns], values[:, columns], scalars[3 + u]
            )

    def out_from(high):
        copies = []
        for group in range(4):
            chunks = pl.ds(4 * group, 4)
            for b in range(4 * group, 4 * group + 4):
                partial[b] = matmul(high[b, 1], context[...]).astype(BF)
            copies.append(
                pltpu.make_async_copy(partial.at[chunks], partial_hbm.at[chunks], sent.at[group])
            )
            copies[-1].start()
        for copy in copies:
            copy.wait()

    def on_first():
        project(normed, other, 0, rest, 0)
        attend_all(mine.at[0], mine.at[1], rest.at[0])
        out_from(other)

    def on_second():
        project(normed, other, 0, rest, 0)
        project(normed, other, 1, rest, 1)
        attend_all(rest.at[0], rest.at[1], mine.at[0])
        out_from(own)

    pl.when(core == 0)(on_first)
    pl.when(core == 1)(on_second)


def combine_kernel(partial, kept, spread, result, sent):
    total = partial[0].astype(F32)
    for head in range(1, CHUNKS):
        total += partial[head].astype(F32)
    result[...] = (kept[...].astype(F32) + total).astype(BF)
    copies = [
        pltpu.make_async_copy(result, spread.at[target], sent.at[target])
        for target in range(CHUNKS)
    ]
    for copy in copies:
        copy.start()
    for copy in copies:
        copy.wait()


def stage_kernel(weights_hbm, staged, arrived):
    copy = pltpu.make_async_copy(weights_hbm.at[:, pl.ds(0, 3)], staged, arrived)
    copy.start()
    copy.wait()


def second_kernel(scalars, x1, weights, gain, rest, packed, normed, qkv):
    rows = []
    gain_rows = gain[...].T
    for u in range(2):
        normalize(x1[:, :, utterance(u)], gain_rows, normed, utterance(u))
    for index in range(3):
        project(normed, weights, index, qkv, index)
    for u in range(2):
        length = scalars[3 + u]
        columns = utterance(u)
        context = attend(qkv[0, :, columns], qkv[1, :, columns], qkv[2, :, columns], length)
        valid = lax.broadcasted_iota(jnp.int32, (128, HD), 0) < length
        total = jnp.where(valid, context.astype(F32).T, F32(0.0))
        pooled = jnp.sum(total, axis=0, keepdims=True) / length.astype(F32)
        rows.append(jnp.concatenate([pooled, rest[u : u + 1, :]], axis=1))
    mine = jnp.concatenate(rows, axis=0)
    for target in range(32):
        packed[target] = mine


def cost(flops, moved):
    return pl.CostEstimate(flops=flops, bytes_accessed=moved, transcendentals=32768)


def run_regroup(lengths, qkv, out):
    return pl.pallas_call(
        regroup_kernel,
        out_shape=pltpu.HBM((2 * NY, 4, 32, HD), BF),
        in_specs=[VMEM, VMEM, VMEM],
        out_specs=pl.BlockSpec(memory_space=pltpu.HBM),
        scratch_shapes=[
            pltpu.VMEM((NY, 4, 32, HD), BF),
            pltpu.SemaphoreType.DMA((2 * NY,)),
        ],
        cost_estimate=cost(0, 400_000),
        name="regroup",
    )(lengths, qkv, out)


def run_input(weights, frames):
    hbm = pl.BlockSpec(memory_space=pltpu.HBM)
    return pl.pallas_call(
        input_kernel,
        out_shape=pltpu.HBM((16, NY, HD, 128), BF),
        in_specs=[hbm, hbm],
        out_specs=hbm,
        scratch_shapes=[
            pltpu.VMEM(weights.shape, BF),
            pltpu.VMEM(frames.shape, BF),
            pltpu.VMEM((NY, HD, 128), BF),
            pltpu.SemaphoreType.DMA((2,)),
            pltpu.SemaphoreType.DMA((16,)),
        ],
        compiler_params=pltpu.CompilerParams(vmem_limit_bytes=20 << 20),
        cost_estimate=cost(100_000_000, 3_000_000),
        name="layer_input",
    )(
        pltpu.with_memory_space_constraint(weights, pltpu.HBM),
        pltpu.with_memory_space_constraint(frames, pltpu.HBM),
    )


def run_norm(scalars, raw, own, gain):
    return pl.pallas_call(
        norm_kernel,
        out_shape=(
            jax.ShapeDtypeStruct((CHUNKS, HD, 256), BF),
            jax.ShapeDtypeStruct((2, HD, 256), BF),
        ),
        in_specs=[SMEM] + [VMEM] * 3,
        out_specs=(VMEM, VMEM),
        compiler_params=pltpu.CompilerParams(vmem_limit_bytes=20 << 20),
        cost_estimate=cost(400_000_000, 4_000_000),
        name="first_norm",
    )(scalars, raw, own, gain)


def run_attend(scalars, raw, normed, mine, own, other):
    return pl.pallas_call(
        attend_kernel,
        out_shape=(
            pltpu.HBM((CHUNKS, HD, 256), BF),
            jax.ShapeDtypeStruct((HD, 256), BF),
        ),
        in_specs=[SMEM] + [VMEM] * 5,
        out_specs=(pl.BlockSpec(memory_space=pltpu.HBM), VMEM),
        scratch_shapes=[
            pltpu.VMEM((2, HD, 256), BF),
            pltpu.VMEM((HD, 256), BF),
            pltpu.VMEM((CHUNKS, HD, 256), BF),
            pltpu.SemaphoreType.DMA((4,)),
        ],
        compiler_params=pltpu.CompilerParams(vmem_limit_bytes=20 << 20),
        cost_estimate=cost(600_000_000, 5_000_000),
        name="first_attend",
    )(scalars, raw, normed, mine, own, other)


def run_combine(partial, kept):
    return pl.pallas_call(
        combine_kernel,
        out_shape=(
            pltpu.HBM((CHUNKS, HD, 256), BF),
            jax.ShapeDtypeStruct((HD, 256), BF),
        ),
        in_specs=[VMEM, VMEM],
        out_specs=(pl.BlockSpec(memory_space=pltpu.HBM), VMEM),
        scratch_shapes=[pltpu.SemaphoreType.DMA((CHUNKS,))],
        compiler_params=pltpu.CompilerParams(vmem_limit_bytes=20 << 20),
        cost_estimate=cost(1_000_000, 2_000_000),
        name="combine",
    )(partial, kept)


def run_stage(weights):
    return pl.pallas_call(
        stage_kernel,
        out_shape=jax.ShapeDtypeStruct((CHUNKS, 3, HD, HD), BF),
        in_specs=[pl.BlockSpec(memory_space=pltpu.HBM)],
        out_specs=VMEM,
        scratch_shapes=[pltpu.SemaphoreType.DMA],
        compiler_params=pltpu.CompilerParams(vmem_limit_bytes=20 << 20),
        cost_estimate=cost(0, 3_000_000),
        name="stage",
    )(weights)


def run_second(scalars, x1, weights, gain, rest):
    return pl.pallas_call(
        second_kernel,
        out_shape=jax.ShapeDtypeStruct((32, 2, 2 * HD), F32),
        in_specs=[SMEM] + [VMEM] * 4,
        out_specs=VMEM,
        scratch_shapes=[
            pltpu.VMEM((CHUNKS, HD, 256), BF),
            pltpu.VMEM((3, HD, 256), BF),
        ],
        compiler_params=pltpu.CompilerParams(vmem_limit_bytes=20 << 20),
        cost_estimate=cost(1_000_000_000, 6_000_000),
        name="second_layer",
    )(scalars, x1, weights, gain, rest)


def body(frames, lengths, feature_proj, norm_gain, qkv_weight, out_weight, center, whitening):
    core = lax.axis_index("c")
    xi, yi = lax.axis_index("x"), lax.axis_index("y")
    chunk = yi * 4 + xi

    projected = run_input(feature_proj.T, frames[0])

    mats = run_regroup(lengths.reshape(1, 1), qkv_weight[0], out_weight[0].T)
    regrouped = lax.all_to_all(mats, ("y", "c"), 0, 0).reshape(NY, 2, 4, 32, HD)
    gains = lax.all_gather(norm_gain[0], "c", axis=0)
    regrouped, gains, projected = lax.optimization_barrier((regrouped, gains, projected))
    plane_lengths = jnp.max(regrouped[:, 0, 0, 30].astype(F32), axis=1).astype(jnp.int32)
    my_lengths = lax.dynamic_slice_in_dim(plane_lengths, 2 * core, 2, 0)

    def shard(layer):
        rows = regrouped[:, layer, :, :30].transpose(1, 0, 2, 3).reshape(4, HD, HD)
        return jnp.concatenate([rows[:3].transpose(0, 2, 1), rows[3:]], axis=0)

    first_shard = lax.dynamic_slice_in_dim(shard(0), 2 * core, 2, 0)
    first_shard, second_shard, my_lengths = lax.optimization_barrier(
        (first_shard, shard(1), my_lengths)
    )
    second_weights = lax.all_gather(second_shard, "z", axis=0)
    own = lax.all_gather(first_shard, "z", axis=0)
    other = swap_cores(own)

    raw = lax.all_to_all(projected, ("y", "x"), 0, 0).reshape(NY, 4, NY, HD, 128)

    scalars = jnp.concatenate([jnp.stack([core, yi, xi]).astype(jnp.int32), my_lengths])
    gains = gains.reshape(2, CHUNKS, HD)
    normed, mine = run_norm(scalars, raw, own, gains[0])
    partial, x0_own = run_attend(scalars, raw, normed, mine, own, other)
    white = whitening.T.reshape(16, CHUNKS, HD).transpose(1, 0, 2)
    x0_own, white = lax.optimization_barrier((x0_own, white))
    near = [(((y + 1 + c) % NY) * 2 + c, y * 2 + c) for y in range(NY) for c in range(2)]
    far = [(((y + 3) % NY) * 2 + 1, y * 2 + 1) for y in range(NY)]
    white_near = lax.ppermute(white, ("y", "c"), near)
    white_far = lax.ppermute(white, ("y", "c"), far)

    partial = lax.all_to_all(partial, ("y", "x"), 0, 0)
    spread, x1_own = run_combine(partial, x0_own)
    x1 = lax.all_to_all(spread, ("y", "x"), 0, 0)

    valid = jnp.arange(128)[None, :] < my_lengths[:, None]
    share = valid.astype(F32) / my_lengths.astype(F32)[:, None]
    pooled_x1 = jnp.sum(x1_own.reshape(HD, 2, 128).astype(F32) * share, axis=2).T
    center_own = lax.dynamic_index_in_dim(center.reshape(CHUNKS, HD), chunk, 0, keepdims=False)
    staged = run_stage(second_weights)
    packed = run_second(scalars, x1, staged, gains[1], pooled_x1 - center_own)

    white_cols = jnp.stack(
        [jnp.where(core == 0, white, white_near), jnp.where(core == 0, white_near, white_far)]
    )
    out_white = jnp.einsum(
        "ybnc,bcr->ynr",
        white_cols,
        second_weights[:, 3].astype(F32),
        precision=lax.Precision.HIGHEST,
    )
    white_own = lax.dynamic_index_in_dim(white_cols, chunk, 1, keepdims=False)
    mixed = jnp.concatenate([out_white, white_own], axis=2)
    swapped = swap_cores(mixed)
    low = jnp.where(core == 0, mixed, swapped)
    high = jnp.where(core == 0, swapped, mixed)
    mixed = jnp.concatenate([low, high, low, high], axis=0)
    mixed = lax.dynamic_slice_in_dim(mixed, (NY - yi) % NY, NY, 0).reshape(64, 2 * HD)

    packed = lax.all_to_all(packed, ("z", "c"), 0, 0).reshape(64, 2 * HD)
    part = jnp.einsum("tk,nk->nt", packed, mixed, precision=lax.Precision.HIGHEST)
    part = part.reshape(NY, 1, 2, 8, 64)
    part = jnp.concatenate([part[:, :, 0], part[:, :, 1]], axis=3)
    part = jnp.broadcast_to(part, (NY, 4, 8, 128)).reshape(16, 8, 128)
    part = lax.all_to_all(part, ("y", "x"), 0, 0)
    total = jnp.sum(part, axis=0)
    return jnp.concatenate([total[:, :64], total[:, 64:]], axis=0).T


def solution(mesh):
    devices = mesh.devices.reshape(-1, NY, 2, 4)
    split = Mesh(devices, ("z", "y", "c", "x"))
    dp = ("z", "y")
    in_specs = (
        P(dp, None, None),
        P(dp),
        P(None, "x"),
        P("c", None),
        P("c", dp, "x"),
        P("c", "x", dp),
        P(),
        P(None, dp),
    )
    return jax.shard_map(
        body, mesh=split, in_specs=in_specs, out_specs=P(None, dp), check_vma=False
    )
```

```python
import jax
import jax.numpy as jnp
from jax import lax
from jax.experimental import pallas as pl
from jax.experimental.pallas import tpu as pltpu
from jax.sharding import Mesh, PartitionSpec as P

HD = 120
NY = 4
CHUNKS = 16
BF = jnp.bfloat16
F32 = jnp.float32
VMEM = pl.BlockSpec(memory_space=pltpu.VMEM)
SMEM = pl.BlockSpec(memory_space=pltpu.SMEM)


def swap_cores(value):
    return lax.ppermute(value, "c", [(0, 1), (1, 0)])


def matmul(left, right):
    return jnp.dot(left, right, preferred_element_type=F32)


def normalize(values, gain_rows, out_ref, columns):
    values = values.astype(F32)
    width = CHUNKS * HD
    mean = jnp.sum(jnp.sum(values, axis=0), axis=0, keepdims=True) / width
    centered = values - mean[None]
    var = jnp.sum(jnp.sum(centered * centered, axis=0), axis=0, keepdims=True) / width
    scale = lax.rsqrt(var + 1e-05)
    for b in range(CHUNKS):
        out_ref[b, :, columns] = (centered[b] * scale * gain_rows[:, b : b + 1]).astype(BF)


def project(normed_ref, weight_ref, index, out_ref, slot):
    total = jnp.zeros((HD, 256), F32)
    for b in range(CHUNKS):
        total += matmul(weight_ref[b, index], normed_ref[b])
    out_ref[slot] = total.astype(BF)


def attend(query, keys, values, length):
    keys = keys.astype(F32).T.astype(BF)
    scores = matmul(keys, query) / jnp.sqrt(F32(HD))
    place = lax.broadcasted_iota(jnp.int32, (128, 128), 0)
    scores = jnp.where(place < length, scores, F32(-1e30))
    top = jnp.max(scores, axis=0, keepdims=True)
    grown = jnp.exp(scores - top)
    probs = (grown / jnp.sum(grown, axis=0, keepdims=True)).astype(BF)
    return matmul(values, probs).astype(BF)


def utterance(u):
    return slice(u * 128, u * 128 + 128)


def regroup_kernel(lengths, qkv, out, mats_hbm, mats, sent):
    tail = jnp.broadcast_to(lengths[...].astype(F32), (2, HD)).astype(BF)
    copies = []
    for y in range(NY):
        for m in range(4):
            start = (m * NY + y) * HD if m < 3 else y * HD
            source = qkv if m < 3 else out
            mats[y, m, 0:30, :] = source[:, start : start + HD]
            mats[y, m, 30:32, :] = tail
        for c in range(2):
            target = 2 * y + c
            copies.append(
                pltpu.make_async_copy(mats.at[y], mats_hbm.at[target], sent.at[target])
            )
            copies[-1].start()
    for copy in copies:
        copy.wait()


def input_kernel(weights_hbm, frames_hbm, spread, weights, frames, blocks, arrived, sent):
    fetches = [
        pltpu.make_async_copy(weights_hbm, weights, arrived.at[0]),
        pltpu.make_async_copy(frames_hbm, frames, arrived.at[1]),
    ]
    for fetch in fetches:
        fetch.start()
    for fetch in fetches:
        fetch.wait()
    projected = lax.dot_general(
        weights[...], frames[...], (((1,), (1,)), ((), ())), preferred_element_type=F32
    )
    for y in range(NY):
        blocks[y] = projected[y * HD : y * HD + HD, :].astype(BF)
    copies = [
        pltpu.make_async_copy(blocks, spread.at[target], sent.at[target]) for target in range(16)
    ]
    for copy in copies:
        copy.start()
    for copy in copies:
        copy.wait()


def norm_kernel(scalars, raw, own, gain, normed, mine):
    core = scalars[0]
    gain_rows = gain[...].T
    for u in range(2):
        picks = [raw[x, 2 * core + u] for x in range(4)]
        values = jnp.concatenate(picks, axis=0)
        normalize(values, gain_rows, normed, utterance(u))
    project(normed, own, 0, mine, 0)
    pl.when(core == 0)(lambda: project(normed, own, 1, mine, 1))


def attend_kernel(
    scalars, raw, normed, mine, own, other, partial_hbm, kept, rest, context, partial, sent
):
    core = scalars[0]
    xi, yi = scalars[1], scalars[2]
    for u in range(2):
        kept[:, utterance(u)] = raw[xi, 2 * core + u, yi]

    def attend_all(query, keys, values):
        for u in range(2):
            columns = utterance(u)
            context[:, columns] = attend(
                query[:, columns], keys[:, columns], values[:, columns], scalars[3 + u]
            )

    def out_from(high):
        copies = []
        for group in range(4):
            chunks = pl.ds(4 * group, 4)
            for b in range(4 * group, 4 * group + 4):
                partial[b] = matmul(high[b, 1], context[...]).astype(BF)
            copies.append(
                pltpu.make_async_copy(partial.at[chunks], partial_hbm.at[chunks], sent.at[group])
            )
            copies[-1].start()
        for copy in copies:
            copy.wait()

    def on_first():
        project(normed, other, 0, rest, 0)
        attend_all(mine.at[0], mine.at[1], rest.at[0])
        out_from(other)

    def on_second():
        project(normed, other, 0, rest, 0)
        project(normed, other, 1, rest, 1)
        attend_all(rest.at[0], rest.at[1], mine.at[0])
        out_from(own)

    pl.when(core == 0)(on_first)
    pl.when(core == 1)(on_second)


def combine_kernel(partial, kept, spread, result, sent):
    total = partial[0].astype(F32)
    for head in range(1, CHUNKS):
        total += partial[head].astype(F32)
    result[...] = (kept[...].astype(F32) + total).astype(BF)
    copies = [
        pltpu.make_async_copy(result, spread.at[target], sent.at[target])
        for target in range(CHUNKS)
    ]
    for copy in copies:
        copy.start()
    for copy in copies:
        copy.wait()


def second_kernel(scalars, x1, weights, gain, rest, packed, normed, qkv):
    rows = []
    gain_rows = gain[...].T
    for u in range(2):
        normalize(x1[:, :, utterance(u)], gain_rows, normed, utterance(u))
    for index in range(3):
        project(normed, weights, index, qkv, index)
    for u in range(2):
        length = scalars[3 + u]
        columns = utterance(u)
        context = attend(qkv[0, :, columns], qkv[1, :, columns], qkv[2, :, columns], length)
        valid = lax.broadcasted_iota(jnp.int32, (128, HD), 0) < length
        total = jnp.where(valid, context.astype(F32).T, F32(0.0))
        pooled = jnp.sum(total, axis=0, keepdims=True) / length.astype(F32)
        rows.append(jnp.concatenate([pooled, rest[u : u + 1, :]], axis=1))
    mine = jnp.concatenate(rows, axis=0)
    for target in range(32):
        packed[target] = mine


def cost(flops, moved):
    return pl.CostEstimate(flops=flops, bytes_accessed=moved, transcendentals=32768)


def run_regroup(lengths, qkv, out):
    return pl.pallas_call(
        regroup_kernel,
        out_shape=pltpu.HBM((2 * NY, 4, 32, HD), BF),
        in_specs=[VMEM, VMEM, VMEM],
        out_specs=pl.BlockSpec(memory_space=pltpu.HBM),
        scratch_shapes=[
            pltpu.VMEM((NY, 4, 32, HD), BF),
            pltpu.SemaphoreType.DMA((2 * NY,)),
        ],
        cost_estimate=cost(0, 400_000),
        name="regroup",
    )(lengths, qkv, out)


def run_input(weights, frames):
    hbm = pl.BlockSpec(memory_space=pltpu.HBM)
    return pl.pallas_call(
        input_kernel,
        out_shape=pltpu.HBM((16, NY, HD, 128), BF),
        in_specs=[hbm, hbm],
        out_specs=hbm,
        scratch_shapes=[
            pltpu.VMEM(weights.shape, BF),
            pltpu.VMEM(frames.shape, BF),
            pltpu.VMEM((NY, HD, 128), BF),
            pltpu.SemaphoreType.DMA((2,)),
            pltpu.SemaphoreType.DMA((16,)),
        ],
        compiler_params=pltpu.CompilerParams(vmem_limit_bytes=20 << 20),
        cost_estimate=cost(100_000_000, 3_000_000),
        name="layer_input",
    )(
        pltpu.with_memory_space_constraint(weights, pltpu.HBM),
        pltpu.with_memory_space_constraint(frames, pltpu.HBM),
    )


def run_norm(scalars, raw, own, gain):
    return pl.pallas_call(
        norm_kernel,
        out_shape=(
            jax.ShapeDtypeStruct((CHUNKS, HD, 256), BF),
            jax.ShapeDtypeStruct((2, HD, 256), BF),
        ),
        in_specs=[SMEM] + [VMEM] * 3,
        out_specs=(VMEM, VMEM),
        compiler_params=pltpu.CompilerParams(vmem_limit_bytes=20 << 20),
        cost_estimate=cost(400_000_000, 4_000_000),
        name="first_norm",
    )(scalars, raw, own, gain)


def run_attend(scalars, raw, normed, mine, own, other):
    return pl.pallas_call(
        attend_kernel,
        out_shape=(
            pltpu.HBM((CHUNKS, HD, 256), BF),
            jax.ShapeDtypeStruct((HD, 256), BF),
        ),
        in_specs=[SMEM] + [VMEM] * 5,
        out_specs=(pl.BlockSpec(memory_space=pltpu.HBM), VMEM),
        scratch_shapes=[
            pltpu.VMEM((2, HD, 256), BF),
            pltpu.VMEM((HD, 256), BF),
            pltpu.VMEM((CHUNKS, HD, 256), BF),
            pltpu.SemaphoreType.DMA((4,)),
        ],
        compiler_params=pltpu.CompilerParams(vmem_limit_bytes=20 << 20),
        cost_estimate=cost(600_000_000, 5_000_000),
        name="first_attend",
    )(scalars, raw, normed, mine, own, other)


def run_combine(partial, kept):
    return pl.pallas_call(
        combine_kernel,
        out_shape=(
            pltpu.HBM((CHUNKS, HD, 256), BF),
            jax.ShapeDtypeStruct((HD, 256), BF),
        ),
        in_specs=[VMEM, VMEM],
        out_specs=(pl.BlockSpec(memory_space=pltpu.HBM), VMEM),
        scratch_shapes=[pltpu.SemaphoreType.DMA((CHUNKS,))],
        compiler_params=pltpu.CompilerParams(vmem_limit_bytes=20 << 20),
        cost_estimate=cost(1_000_000, 2_000_000),
        name="combine",
    )(partial, kept)


def run_second(scalars, x1, weights, gain, rest):
    return pl.pallas_call(
        second_kernel,
        out_shape=jax.ShapeDtypeStruct((32, 2, 2 * HD), F32),
        in_specs=[SMEM] + [VMEM] * 4,
        out_specs=VMEM,
        scratch_shapes=[
            pltpu.VMEM((CHUNKS, HD, 256), BF),
            pltpu.VMEM((3, HD, 256), BF),
        ],
        compiler_params=pltpu.CompilerParams(vmem_limit_bytes=20 << 20),
        cost_estimate=cost(1_000_000_000, 6_000_000),
        name="second_layer",
    )(scalars, x1, weights, gain, rest)


def body(frames, lengths, feature_proj, norm_gain, qkv_weight, out_weight, center, whitening):
    core = lax.axis_index("c")
    xi, yi = lax.axis_index("x"), lax.axis_index("y")
    chunk = xi * NY + yi

    projected = run_input(feature_proj.T, frames[0])

    mats = run_regroup(lengths.reshape(1, 1), qkv_weight[0], out_weight[0].T)
    regrouped = lax.all_to_all(mats, ("y", "c"), 0, 0).reshape(NY, 2, 4, 32, HD)
    gains = lax.all_gather(norm_gain[0], "c", axis=0)
    regrouped, gains, projected = lax.optimization_barrier((regrouped, gains, projected))
    plane_lengths = jnp.max(regrouped[:, 0, 0, 30].astype(F32), axis=1).astype(jnp.int32)
    my_lengths = lax.dynamic_slice_in_dim(plane_lengths, 2 * core, 2, 0)

    rows = regrouped[:, 0, :, :30].transpose(1, 0, 2, 3).reshape(4, HD, HD)
    rows = jnp.concatenate([rows[:3].transpose(0, 2, 1), rows[3:]], axis=0)
    first_shard = lax.dynamic_slice_in_dim(rows, 2 * core, 2, 0)
    gathered = lax.all_gather(regrouped[:, 1], "z", axis=0)[:, :, :, :30]
    gathered = gathered.transpose(0, 2, 1, 3, 4).reshape(CHUNKS, 4, HD, HD)
    second_qkv = gathered[:, :3].transpose(0, 1, 3, 2)
    second_out = gathered[:, 3]
    own = lax.all_gather(first_shard, "z", axis=0)
    other = swap_cores(own)

    raw = lax.all_to_all(projected, ("x", "y"), 0, 0).reshape(4, NY, NY, HD, 128)

    scalars = jnp.concatenate([jnp.stack([core, xi, yi]).astype(jnp.int32), my_lengths])
    gains = gains.reshape(2, CHUNKS, HD)
    normed, mine = run_norm(scalars, raw, own, gains[0])
    partial, x0_own = run_attend(scalars, raw, normed, mine, own, other)
    white = whitening.T.reshape(16, CHUNKS, HD).transpose(1, 0, 2)
    x0_own, white = lax.optimization_barrier((x0_own, white))
    near = [(((y + 1 + c) % NY) * 2 + c, y * 2 + c) for y in range(NY) for c in range(2)]
    far = [(((y + 3) % NY) * 2 + 1, y * 2 + 1) for y in range(NY)]
    white_near = lax.ppermute(white, ("y", "c"), near)
    white_far = lax.ppermute(white, ("y", "c"), far)

    partial = lax.all_to_all(partial, ("x", "y"), 0, 0)
    spread, x1_own = run_combine(partial, x0_own)
    x1 = lax.all_to_all(spread, ("x", "y"), 0, 0)

    valid = jnp.arange(128)[None, :] < my_lengths[:, None]
    share = valid.astype(F32) / my_lengths.astype(F32)[:, None]
    pooled_x1 = jnp.sum(x1_own.reshape(HD, 2, 128).astype(F32) * share, axis=2).T
    center_own = lax.dynamic_index_in_dim(center.reshape(CHUNKS, HD), chunk, 0, keepdims=False)
    packed = run_second(scalars, x1, second_qkv, gains[1], pooled_x1 - center_own)

    white_cols = jnp.stack(
        [jnp.where(core == 0, white, white_near), jnp.where(core == 0, white_near, white_far)]
    )
    out_white = jnp.einsum(
        "ybnc,bcr->ynr",
        white_cols,
        second_out.astype(F32),
        precision=lax.Precision.HIGHEST,
    )
    white_own = lax.dynamic_index_in_dim(white_cols, chunk, 1, keepdims=False)
    mixed = jnp.concatenate([out_white, white_own], axis=2)
    swapped = swap_cores(mixed)
    low = jnp.where(core == 0, mixed, swapped)
    high = jnp.where(core == 0, swapped, mixed)
    mixed = jnp.concatenate([low, high, low, high], axis=0)
    mixed = lax.dynamic_slice_in_dim(mixed, (NY - yi) % NY, NY, 0).reshape(64, 2 * HD)

    packed = lax.all_to_all(packed, ("z", "c"), 0, 0).reshape(64, 2 * HD)
    part = jnp.einsum("tk,nk->nt", packed, mixed, precision=lax.Precision.HIGHEST)
    part = part.reshape(NY, 1, 2, 8, 64)
    part = jnp.concatenate([part[:, :, 0], part[:, :, 1]], axis=3)
    part = jnp.broadcast_to(part, (NY, 4, 8, 128)).reshape(16, 8, 128)
    part = lax.all_to_all(part, ("y", "x"), 0, 0)
    total = jnp.sum(part, axis=0)
    return jnp.concatenate([total[:, :64], total[:, 64:]], axis=0).T


def solution(mesh):
    devices = mesh.devices.reshape(-1, NY, 2, 4)
    split = Mesh(devices, ("z", "y", "c", "x"))
    dp = ("z", "y")
    in_specs = (
        P(dp, None, None),
        P(dp),
        P(None, "x"),
        P("c", None),
        P("c", dp, "x"),
        P("c", "x", dp),
        P(),
        P(None, dp),
    )
    return jax.shard_map(
        body, mesh=split, in_specs=in_specs, out_specs=P(None, dp), check_vma=False
    )
```
